256 devices in a mesh: gx: 32 (over z_hi, x, y), gy: 2 (over core), gz: 4 (over z_lo).
Axes of the slice: x: 4, y: 4, z: 8 (z_hi: 2, z_lo: 4; z = z_hi * 4 + z_lo), core: 2. Of those that a mesh axis runs over, the one named last changes fastest.
Arguments:
- flow_state: float32 [4, 128, 64, 512], P(None, 'gx', 'gy', 'gz'), may hold values from -6 to 6
- viscosity: float32 [4, 128, 64, 512], P(None, 'gx', 'gy', 'gz'), may hold values from 0.05 to 0.5
- lift_weight: float32 [8, 128], replicated, may hold values from -6 to 6
- lift_bias: float32 [128], replicated, may hold values from -2 to 2
- norm_gains: float32 [6, 128], replicated, may hold values from 0.1 to 1.9
- query_weight: bfloat16 [2, 128, 128], replicated, may hold values from -4 to 4
- key_weight: bfloat16 [2, 128, 128], replicated, may hold values from -4 to 4
- value_weight: bfloat16 [2, 128, 128], replicated, may hold values from -0.5 to 0.5
- output_weight: bfloat16 [2, 128, 128], replicated, may hold values from -0.5 to 0.5
- up_weight: bfloat16 [2, 128, 512], replicated, may hold values from -0.5 to 0.5
- down_weight: bfloat16 [2, 512, 128], replicated, may hold values from -0.25 to 0.25
- head_weight: bfloat16 [128, 4], replicated, may hold values from -1.5 to 1.5
Outputs:
- state_next: float32 [4, 128, 64, 512], P(None, 'gx', 'gy', 'gz')
- eddy_field: float32 [4, 128, 64, 512], P(None, 'gx', 'gy', 'gz')
The draws below stay inside these ranges and needn't reach their ends.
All inputs are finite; a program needn't handle non-finite values.
Results may differ from the reference program's by a relative error of at most 0.0058.
The reference program's roundings to bfloat16 on the way count: a program that leaves them out, or rounds other values in their place, can miss the bound.
Values may be sent and summed in bfloat16 or wider, within the bound.
A program may use at most 64 MiB of HBM per device.

```python
import math
import jax
import jax.numpy as jnp
from jax import lax

FIELDS = 4
D = 128
HID = 512
NX = 128
NY = 64
NZ = 512


def draw_query_weight(key, part):
    private_part = jax.random.normal(jax.random.fold_in(key, 1), (2, D, D), jnp.float32) * D ** (-0.5)
    return jnp.clip(private_part, -4.0, 4.0).astype(jnp.bfloat16)


def draw_key_weight(key, part):
    private_part = jax.random.normal(jax.random.fold_in(key, 2), (2, D, D), jnp.float32) * D ** (-0.5)
    return jnp.clip(private_part, -4.0, 4.0).astype(jnp.bfloat16)


def block_scale(key, shape, split, least, high):
    level, own = 1.0, jax.random.fold_in(key, 6)
    for dim, parts in split:
        steps = jnp.exp(jax.random.uniform(jax.random.fold_in(own, dim), (parts,), jnp.float32, least / len(split), high / len(split)))
        level = level * jnp.repeat(steps, shape[dim] // parts).reshape([-1 if axis == dim else 1 for axis in range(len(shape))])
    return level


def centred(stream_key, shape, scale, most, split=(), kind=jnp.bfloat16):
    level = block_scale(stream_key, shape, split, -0.22, 0.18) if split else 1.0
    drawn = jax.random.normal(stream_key, shape, jnp.float32) * scale * level
    return jnp.minimum(jnp.maximum(drawn, -most), most).astype(kind)


def setup_inputs(seed: int = 0) -> dict:
    splits = jax.random.split(jax.random.key(seed), 13)
    flow_state = centred(splits[0], (FIELDS, NX, NY, NZ), 1.0, 6.0, ((1, 32), (2, 2), (3, 4)), jnp.float32)
    viscosity = jnp.clip(jnp.exp(math.log(0.5) - 2.3025851 * jax.random.uniform(splits[1], (FIELDS, NX, NY, NZ), jnp.float32) ** block_scale(splits[1], (FIELDS, NX, NY, NZ), ((1, 32), (2, 2), (3, 4)), -0.2, 0.2)), 0.05, 0.5)
    lift_weight = centred(splits[2], (2 * FIELDS, D), 1 ** -0.5, 6.0, (), jnp.float32)
    lift_bias = centred(splits[3], (D,), 0.5, 2.0, (), jnp.float32)
    norm_gains = jnp.clip(1.0 + 0.18 * jax.random.normal(splits[4], (6, D), jnp.float32), 0.1, 1.9)
    query_weight = draw_query_weight(jax.random.fold_in(splits[12], 71), 0)
    key_weight = draw_key_weight(jax.random.fold_in(splits[12], 71), 0)
    value_weight = centred(splits[7], (2, D, D), D ** -0.5, 0.5)
    output_weight = centred(splits[8], (2, D, D), D ** -0.5, 0.5)
    up_weight = centred(splits[9], (2, D, HID), D ** -0.5, 0.5)
    down_weight = centred(splits[10], (2, HID, D), HID ** -0.5, 0.25)
    head_weight = centred(splits[11], (D, FIELDS), (D // 8) ** -0.5, 1.5)
    return dict(flow_state=flow_state, viscosity=viscosity, lift_weight=lift_weight, lift_bias=lift_bias, norm_gains=norm_gains, query_weight=query_weight, key_weight=key_weight, value_weight=value_weight, output_weight=output_weight, up_weight=up_weight, down_weight=down_weight, head_weight=head_weight)


EPSILON = 1e-06
TIME_STEP = 0.3

def window(source, which_axis, offset):
    slicers = [slice(None), slice(1, -1), slice(1, -1), slice(1, -1)]
    slicers[which_axis] = slice(1 + offset, source.shape[which_axis] - 1 + offset)
    return source[tuple(slicers)]

def tendency(fields, viscous):
    middle = window(fields, 1, 0)
    nu_middle = window(viscous, 1, 0)
    summed = jnp.zeros_like(middle)
    for which_axis in (1, 2, 3):
        forward = window(fields, which_axis, 1)
        backward = window(fields, which_axis, -1)
        nu_forward = 0.5 * (nu_middle + window(viscous, which_axis, 1))
        nu_backward = 0.5 * (nu_middle + window(viscous, which_axis, -1))
        velocity = middle[which_axis - 1][None]
        summed = summed - velocity * (0.5 * (forward - backward)) + nu_forward * (forward - middle) - nu_backward * (middle - backward)
    return summed

def periodic(source):
    return jnp.pad(source, ((0, 0), (1, 1), (1, 1), (1, 1)), mode='wrap')

def coarsen(source):
    shaped = source.reshape(source.shape[0], source.shape[1] // 2, 2, source.shape[2] // 2, 2, source.shape[3] // 2, 2)
    return lax.optimization_barrier(jnp.mean(shaped, axis=(2, 4, 6)))

def refine(padded, which_axis):
    extent = padded.shape[which_axis]
    center = lax.slice_in_dim(padded, 1, extent - 1, axis=which_axis)
    behind = lax.slice_in_dim(padded, 0, extent - 2, axis=which_axis)
    forward = lax.slice_in_dim(padded, 2, extent, axis=which_axis)
    lower_half = 0.75 * center + 0.25 * behind
    upper_half = 0.75 * center + 0.25 * forward
    paired = jnp.stack([lower_half, upper_half], axis=which_axis + 1)
    new_shape = list(center.shape)
    new_shape[which_axis] = 2 * new_shape[which_axis]
    return paired.reshape(new_shape)

def rms_scale(values, scaling):
    return values * lax.rsqrt(lax.optimization_barrier(jnp.mean(values * values, axis=-1, keepdims=True)) + EPSILON) * scaling

def matmul(values, matrix):
    flat_rows = values.reshape(-1, values.shape[-1])
    product = jnp.dot(flat_rows, matrix, preferred_element_type=jnp.float32)
    return product.reshape(values.shape[:-1] + (matrix.shape[-1],))

def mixer(section, along_axis, weights, gain_pair):
    query_matrix, key_matrix, value_matrix, output_matrix, up_matrix, down_matrix = weights
    carried = section.astype(jnp.float32)
    normed = rms_scale(carried, gain_pair[0]).astype(jnp.bfloat16)
    queries = matmul(normed, query_matrix).astype(jnp.bfloat16)
    key_rows = matmul(normed, key_matrix).astype(jnp.bfloat16)
    value_rows = matmul(normed, value_matrix).astype(jnp.bfloat16)
    if along_axis == 0:
        scores = jnp.einsum('lnd,mnd->nlm', queries.astype(jnp.float32), key_rows.astype(jnp.float32))
    else:
        scores = jnp.einsum('nld,nmd->nlm', queries.astype(jnp.float32), key_rows.astype(jnp.float32))
    scores = scores * queries.shape[-1] ** (-0.5)
    scores = scores - lax.optimization_barrier(jnp.max(scores, axis=-1, keepdims=True))
    exponent = jnp.exp(scores)
    attention = (exponent / lax.optimization_barrier(jnp.sum(exponent, axis=-1, keepdims=True))).astype(jnp.bfloat16)
    if along_axis == 0:
        attended = jnp.einsum('nlm,mnd->lnd', attention.astype(jnp.float32), value_rows.astype(jnp.float32))
    else:
        attended = jnp.einsum('nlm,nmd->nld', attention.astype(jnp.float32), value_rows.astype(jnp.float32))
    attended = attended.astype(jnp.bfloat16)
    residual = carried + matmul(attended, output_matrix)
    normed_again = rms_scale(residual, gain_pair[1]).astype(jnp.bfloat16)
    hidden = jax.nn.gelu(matmul(normed_again, up_matrix)).astype(jnp.bfloat16)
    return (residual + matmul(hidden, down_matrix)).astype(jnp.bfloat16)

def advance(flow_state, viscosity):
    viscous_wide = periodic(viscosity)
    segment_one = flow_state + TIME_STEP * tendency(periodic(flow_state), viscous_wide)
    segment_two = 0.75 * flow_state + 0.25 * (segment_one + TIME_STEP * tendency(periodic(segment_one), viscous_wide))
    return flow_state / 3.0 + 2.0 / 3.0 * (segment_two + TIME_STEP * tendency(periodic(segment_two), viscous_wide))

def reference(flow_state, viscosity, lift_weight, lift_bias, norm_gains, query_weight, key_weight, value_weight, output_weight, up_weight, down_weight, head_weight):
    state_next = advance(flow_state, viscosity)
    filtered = jnp.concatenate([coarsen(state_next), coarsen(state_next * state_next)], axis=0)
    channels, first_extent, second_extent, third_extent = filtered.shape
    group_size = math.gcd(third_extent, 4)
    grouped = filtered.reshape(channels, first_extent, second_extent, third_extent // group_size, group_size)
    grouped = jnp.transpose(grouped, (3, 0, 1, 4, 2))
    first_weights = (query_weight[0], key_weight[0], value_weight[0], output_weight[0], up_weight[0], down_weight[0])
    second_weights = (query_weight[1], key_weight[1], value_weight[1], output_weight[1], up_weight[1], down_weight[1])

    def column_group(block_input):
        lifted = jnp.einsum('cxzy,cd->xzyd', block_input, lift_weight, precision=lax.Precision.HIGHEST) + lift_bias
        features = jax.nn.gelu(rms_scale(lifted, norm_gains[0])).astype(jnp.bfloat16)
        first_pass = mixer(features.reshape(first_extent, group_size * second_extent, D), 0, first_weights, norm_gains[1:3])
        second_pass = mixer(first_pass.reshape(first_extent * group_size, second_extent, D), 1, second_weights, norm_gains[3:5])
        final_norm = rms_scale(second_pass.astype(jnp.float32), norm_gains[5]).astype(jnp.bfloat16)
        coefficient = 0.05 + 0.45 * jax.nn.sigmoid(matmul(final_norm, head_weight))
        return coefficient.reshape(first_extent, group_size, second_extent, FIELDS)
    coarse_eddy = lax.map(column_group, grouped)
    coarse_eddy = jnp.transpose(coarse_eddy, (4, 1, 3, 0, 2)).reshape(FIELDS, first_extent, second_extent, third_extent)
    eddy_field = refine(refine(refine(periodic(coarse_eddy), 3), 2), 1)
    return (state_next, eddy_field)
```

```python
import functools
import math

import jax
import jax.numpy as jnp
from jax import lax
from jax.experimental import pallas as pl
from jax.experimental.pallas import tpu as pltpu
from jax.sharding import PartitionSpec as P

EPSILON = 1e-06
TIME_STEP = 0.3
MESH = pl.DeviceIdType.MESH
F32 = jnp.float32
BF16 = jnp.bfloat16
DMA = pltpu.SemaphoreType.DMA
HIGHEST = lax.Precision.HIGHEST


def iota(shape, dim):
    return lax.broadcasted_iota(jnp.int32, shape, dim)


def rms(values, gain):
    square = jnp.mean(values * values, axis=-1, keepdims=True)
    return values * lax.rsqrt(square + EPSILON) * gain


def gelu(values):
    inner = math.sqrt(2.0 / math.pi) * (values + 0.044715 * (values * values * values))
    return 0.5 * values * (1.0 + jnp.tanh(inner))


def dot(left, right):
    return jnp.dot(left, right, preferred_element_type=F32)


def dot_nt(left, right, precision=None):
    return lax.dot_general(
        left, right, (((1,), (1,)), ((), ())), precision=precision, preferred_element_type=F32
    )


def order4(step):
    return lax.rem(2 + 3 * step + 3 * (step // 2) + 2 * (step // 3), 4)


def peer(step, gx, gy):
    tz = lax.rem(gx // 16 + 1 + step // 32, 2)
    tx = lax.rem(lax.rem(gx // 4, 4) + order4(lax.rem(step // 8, 4)), 4)
    ty = lax.rem(lax.rem(gx, 4) + order4(lax.rem(step // 2, 4)), 4)
    tc = lax.rem(gy + 1 + lax.rem(step, 2), 2)
    return tz * 16 + tx * 4 + ty, tc


def mixer(carried, mask, gains, weights):
    groups, rows, width = carried.shape
    query, key, value, out, up, down = weights
    flat = carried.reshape(groups * rows, width)
    normed = rms(flat, gains[0]).astype(BF16)
    queries = dot(normed, query).astype(BF16)
    keys = dot(normed, key).astype(BF16)
    values = dot(normed, value).astype(BF16)
    pieces = []
    for g in range(groups):
        part = slice(g * rows, (g + 1) * rows)
        scores = dot_nt(queries[part], keys[part]) * (width**-0.5)
        scores = jnp.where(mask, scores, -1e30)
        exponent = jnp.exp(scores - jnp.max(scores, axis=-1, keepdims=True))
        attention = exponent * (1.0 / jnp.sum(exponent, axis=-1, keepdims=True))
        pieces.append(dot(attention.astype(BF16), values[part]).astype(BF16))
    attended = jnp.concatenate(pieces, axis=0) if groups > 1 else pieces[0]
    residual = flat + dot(attended, out)
    again = rms(residual, gains[1]).astype(BF16)
    hidden = gelu(dot(again, up)).astype(BF16)
    return (residual + dot(hidden, down)).astype(BF16)


def main_kernel(
    state_hbm, visc_hbm, lift_hbm, bias_hbm, gains_hbm, query_hbm, key_hbm, value_hbm, out_hbm,
    up_hbm, down_hbm, head_hbm,
    next_hbm, coarse_hbm,
    s0, s1, s2, s3, visc, nu_f, nu_b, nu_sum, xs, xr, ys, yr, zs, zr, pool, filt, recv, hid, cbuf,
    ebuf, lift_w, bias_w, gains_w, query_w, key_w, value_w, out_w, up_w, down_w, head_w,
    load_sem, weight_sem, face_send, face_recv, a_send, a_recv, b_send, b_recv, edge_send, out_sem,
):
    gx, gy, gz = lax.axis_index("gx"), lax.axis_index("gy"), lax.axis_index("gz")
    plane = gx * 2 + gy
    loads = []
    for x in range(4):
        for n, (src, dst) in enumerate(((state_hbm, s0), (visc_hbm, visc))):
            loads.append(pltpu.make_async_copy(src.at[:, x], dst.at[x], load_sem.at[n, x]))
            loads[-1].start()
    weight_pairs = (
        (lift_hbm, lift_w), (bias_hbm, bias_w), (gains_hbm, gains_w), (query_hbm, query_w),
        (key_hbm, key_w), (value_hbm, value_w), (out_hbm, out_w), (up_hbm, up_w),
        (down_hbm, down_w), (head_hbm, head_w),
    )
    weight_loads = []
    for n, (src, dst) in enumerate(weight_pairs):
        weight_loads.append(pltpu.make_async_copy(src, dst, weight_sem.at[n]))
        weight_loads[-1].start()

    barrier = pltpu.get_barrier_semaphore()

    def greet(step, carry):
        tx, ty = peer(step, gx, gy)
        pl.semaphore_signal(barrier, inc=1, device_id={"gx": tx, "gy": ty}, device_id_type=MESH)
        return carry

    z_next, z_last = lax.rem(gz + 1, 4), lax.rem(gz + 3, 4)
    lax.fori_loop(0, 63, greet, 0)
    for target in (z_next, z_last):
        pl.semaphore_signal(barrier, inc=1, device_id={"gz": target}, device_id_type=MESH)
    pl.semaphore_signal(
        barrier, inc=1, device_id={"gx": 0, "gy": 0, "gz": z_next}, device_id_type=MESH
    )
    pl.semaphore_signal(
        barrier, inc=1, device_id={"gx": 31, "gy": 1, "gz": z_last}, device_id_type=MESH
    )

    for copy in loads:
        copy.wait()

    lanes32 = iota((32, 128), 1)

    def stage(e, source):
        xs[e, 0] = source[0].astype(BF16)
        xs[e, 1] = source[3].astype(BF16)
        packed = jnp.zeros((32, 128), F32)
        for x in range(4):
            for f in range(4):
                j = x * 4 + f
                ys[e, 0, j : j + 1, :] = source[x, f, 0:1, :]
                ys[e, 1, j : j + 1, :] = source[x, f, 31:32, :]
                block = source[x, f]
                packed = jnp.where(lanes32 == j, block[:, 0:1], packed)
                packed = jnp.where(lanes32 == 16 + j, block[:, 127:128], packed)
        zs[e] = packed

    x_next, x_last = lax.rem(gx + 1, 32), lax.rem(gx + 31, 32)

    def face_copies(e):
        pairs = (
            (xs.at[e, 1], xr.at[e, 0], {"gx": x_next}),
            (xs.at[e, 0], xr.at[e, 1], {"gx": x_last}),
            (zs.at[e], zr.at[e, 0], {"gz": z_next}),
            (zs.at[e], zr.at[e, 1], {"gz": z_last}),
            (ys.at[e], yr.at[e], {"gy": 1 - gy}),
        )
        return [
            pltpu.make_async_remote_copy(
                src_ref=src, dst_ref=dst, send_sem=face_send.at[e, n], recv_sem=face_recv.at[e, n],
                device_id=device, device_id_type=MESH,
            )
            for n, (src, dst, device) in enumerate(pairs)
        ]

    stage(0, s0)
    stage(1, visc)
    extra = jnp.where(plane == 0, 64, 0) + jnp.where(plane == 63, 64, 0)
    pl.semaphore_wait(barrier, 65 + extra)
    copies = [face_copies(e) for e in range(4)]
    for e in range(2):
        for copy in copies[e]:
            copy.start()

    rows = iota((128, 128), 0)
    lanes = iota((128, 128), 1)
    row32 = lax.rem(rows, 32)

    def neighbours(e, source, x):
        middle = source[x].reshape(128, 128)
        if x == 0:
            x_b = xr[e, 0].astype(F32).reshape(128, 128)
        else:
            x_b = source[x - 1].reshape(128, 128)
        if x == 3:
            x_f = xr[e, 1].astype(F32).reshape(128, 128)
        else:
            x_f = source[x + 1].reshape(128, 128)

        def spread(side):
            return jnp.concatenate(
                [
                    jnp.broadcast_to(yr[e, side, x * 4 + f : x * 4 + f + 1, :], (32, 128))
                    for f in range(4)
                ],
                axis=0,
            )

        y_b = jnp.where(row32 == 0, spread(1), pltpu.roll(middle, 1, 0))
        y_f = jnp.where(row32 == 31, spread(0), pltpu.roll(middle, 127, 0))

        def column(side, first):
            return jnp.concatenate(
                [
                    jnp.broadcast_to(
                        zr[e, side, :, first + x * 4 + f : first + x * 4 + f + 1], (32, 128)
                    )
                    for f in range(4)
                ],
                axis=0,
            )

        z_b = jnp.where(lanes == 0, column(0, 16), pltpu.roll(middle, 1, 1))
        z_f = jnp.where(lanes == 127, column(1, 0), pltpu.roll(middle, 127, 1))
        return middle, ((x_b, x_f), (y_b, y_f), (z_b, z_f))

    def advance(e, source, combine):
        for x in range(4):
            middle, pairs = neighbours(e, source, x)
            total = -middle * nu_sum[x]
            for d, (before, after) in enumerate(pairs):
                half = (0.5 * TIME_STEP) * source[x, d]
                half = jnp.concatenate([half] * 4, axis=0)
                total += after * (nu_f[d, x] - half) + before * (nu_b[d, x] + half)
            combine(x, middle + total)

    for copy in copies[1]:
        copy.wait_recv()
    for x in range(4):
        middle, pairs = neighbours(1, visc, x)
        total = jnp.zeros((128, 128), F32)
        for d, (before, after) in enumerate(pairs):
            forward = (0.5 * TIME_STEP) * (middle + after)
            backward = (0.5 * TIME_STEP) * (middle + before)
            nu_f[d, x] = forward
            nu_b[d, x] = backward
            total += forward + backward
        nu_sum[x] = total

    def first(x, value):
        s1[x] = value.reshape(4, 32, 128)

    def second(x, value):
        s2[x] = (0.75 * s0[x].reshape(128, 128) + 0.25 * value).reshape(4, 32, 128)

    def third(x, value):
        s3[x] = (s0[x].reshape(128, 128) / 3.0 + (2.0 / 3.0) * value).reshape(4, 32, 128)

    for copy in copies[0]:
        copy.wait_recv()
    advance(0, s0, first)
    stage(2, s1)
    for copy in copies[2]:
        copy.start()
    for copy in copies[2]:
        copy.wait_recv()
    advance(2, s1, second)
    stage(3, s2)
    for copy in copies[3]:
        copy.start()
    for copy in copies[3]:
        copy.wait_recv()
    advance(3, s2, third)

    results = []
    for x in range(4):
        results.append(pltpu.make_async_copy(s3.at[x], next_hbm.at[:, x], out_sem.at[x]))
        results[-1].start()

    pick = jnp.where(iota((64, 128), 1) // 2 == iota((64, 128), 0), 0.125, 0.0)
    for x in range(2):
        one, two = s3[2 * x].reshape(128, 128), s3[2 * x + 1].reshape(128, 128)
        pool[x, 0:128] = one + two
        pool[x, 128:256] = one * one + two * two
        paired = pool[x, pl.ds(0, 128, stride=2), :] + pool[x, pl.ds(1, 128, stride=2), :]
        filt[:, x, :] = dot_nt(pick, paired, HIGHEST)

    def send_filtered(step, carry):
        tx, ty = peer(step, gx, gy)
        pltpu.make_async_remote_copy(
            src_ref=filt.at[tx * 2 + ty], dst_ref=recv.at[gy * 32 + gx], send_sem=a_send,
            recv_sem=a_recv, device_id={"gx": tx, "gy": ty}, device_id_type=MESH,
        ).start()
        return carry

    lax.fori_loop(0, 63, send_filtered, 0)
    recv[pl.ds(gy * 32 + gx, 1)] = filt[pl.ds(plane, 1)]

    for copy in weight_loads:
        copy.wait()
    lift_rows = jnp.concatenate(
        [jnp.broadcast_to(lift_w[c : c + 1, :], (16, 128)) for c in range(8)], axis=0
    )
    head_lanes = jnp.concatenate(
        [jnp.broadcast_to(head_w[:, f : f + 1].astype(F32), (128, 32)) for f in range(4)], axis=1
    ).astype(BF16)

    a_all = pltpu.make_async_remote_copy(
        src_ref=filt.at[pl.ds(0, 63)], dst_ref=recv.at[pl.ds(0, 63)], send_sem=a_send,
        recv_sem=a_recv, device_id={"gy": 1 - gy}, device_id_type=MESH,
    )
    a_all.wait_recv()

    filtered = jnp.concatenate([recv[:, 0, :], recv[:, 1, :]], axis=0)
    along_x = lax.rem(rows // 32, 2) == lax.rem(lanes // 32, 2)
    lane16 = lax.rem(lanes, 16)

    def block_weights(i):
        return (query_w[i], key_w[i], value_w[i], out_w[i], up_w[i], down_w[i])

    def gain(i):
        return gains_w[i : i + 1, :]

    GROUP = 4

    def x_block(step, carry):
        inputs = jnp.concatenate(
            [jnp.where(lane16 == step * GROUP + g, filtered, 0.0) for g in range(GROUP)], axis=0
        )
        lifted = (
            jnp.dot(inputs, lift_rows, precision=HIGHEST, preferred_element_type=F32) + bias_w[...]
        )
        features = gelu(rms(lifted, gain(0))).astype(BF16).astype(F32)
        result = mixer(
            features.reshape(GROUP, 128, 128), along_x, (gain(1), gain(2)), block_weights(0)
        )
        hid[pl.ds(step * GROUP, GROUP)] = result.astype(F32).reshape(GROUP, 2, 2, 32, 128)
        return carry

    lax.fori_loop(0, 16 // GROUP, x_block, 0)

    along_y = lax.rem(iota((256, 256), 0), 8) == lax.rem(iota((256, 256), 1), 8)
    cell = iota((32, 8, 128), 0)
    own_lane = lax.rem(iota((32, 8, 128), 2), 32) == lax.rem(cell, 2) * 16 + cell // 2

    def y_block(x, g):
        lines = hid[:, x, :, 8 * g : 8 * g + 8, :].reshape(1, 256, 128)
        result = mixer(lines, along_y, (gain(3), gain(4)), block_weights(1))
        final = rms(result.astype(F32), gain(5)).astype(BF16)
        spread = dot(final, head_lanes).reshape(32, 8, 128)
        logits = jnp.sum(jnp.where(own_lane, spread, 0.0), axis=0)
        coefficient = 0.05 + 0.45 * (1.0 / (1.0 + jnp.exp(-logits)))
        for r in range(8):
            cbuf[1 + x + 2 * (8 * g + r)] = coefficient[r : r + 1, :]

    for x in range(2):
        for g in range(4):
            y_block(x, g)
    cbuf[0] = cbuf[64]
    cbuf[65] = cbuf[1]

    def send_coarse(step, carry):
        tx, ty = peer(step, gx, gy)
        pltpu.make_async_remote_copy(
            src_ref=cbuf.at[pl.ds(2 * tx, 4)], dst_ref=ebuf.at[plane + 1], send_sem=b_send,
            recv_sem=b_recv, device_id={"gx": tx, "gy": ty}, device_id_type=MESH,
        ).start()
        return carry

    def send_edge(slot, target_z, step, carry):
        tx, ty = peer(step, gx, gy)
        pltpu.make_async_remote_copy(
            src_ref=cbuf.at[pl.ds(2 * tx, 4)], dst_ref=ebuf.at[slot], send_sem=edge_send,
            recv_sem=b_recv, device_id={"gx": tx, "gy": ty, "gz": target_z}, device_id_type=MESH,
        ).start()
        return carry

    @pl.when(plane == 63)
    def _():
        lax.fori_loop(0, 64, functools.partial(send_edge, 0, z_next), 0)

    @pl.when(plane == 0)
    def _():
        lax.fori_loop(0, 64, functools.partial(send_edge, 65, z_last), 0)

    lax.fori_loop(0, 63, send_coarse, 0)
    ebuf[pl.ds(plane + 1, 1)] = cbuf[pl.ds(2 * gx, 4)].reshape(1, 4, 1, 128)
    ebuf[66:72] = jnp.zeros((6, 4, 1, 128), F32)
    b_all = pltpu.make_async_remote_copy(
        src_ref=ebuf.at[pl.ds(0, 63)], dst_ref=ebuf.at[pl.ds(0, 65)], send_sem=b_send,
        recv_sem=b_recv, device_id={"gy": 1 - gy}, device_id_type=MESH,
    )
    b_all.wait_recv()
    final_copy = pltpu.make_async_copy(ebuf, coarse_hbm, out_sem.at[4])
    final_copy.start()
    for e in range(4):
        for copy in copies[e]:
            copy.wait_send()
    a_all.wait_send()
    b_all.wait_send()

    @pl.when((plane == 63) | (plane == 0))
    def _():
        pltpu.make_async_remote_copy(
            src_ref=ebuf.at[pl.ds(0, 64)], dst_ref=ebuf.at[pl.ds(0, 64)], send_sem=edge_send,
            recv_sem=b_recv, device_id={"gy": 1 - gy}, device_id_type=MESH,
        ).wait_send()

    for copy in results:
        copy.wait()
    final_copy.wait()


def refine_kernel(next_in, coarse, next_out, eddy, sem):
    copy = pltpu.make_async_copy(next_in, next_out, sem)
    copy.start()
    gy = lax.axis_index("gy")
    row, column = iota((128, 128), 0), iota((128, 128), 1)
    fine = lax.rem(column, 32)
    centre = gy * 16 + fine // 2
    other = lax.rem(centre + 31 + 2 * lax.rem(fine, 2), 32)
    same = row // 32 == column // 32
    along_y = jnp.where(same & (lax.rem(row, 32) == centre), 0.75, 0.0) + jnp.where(
        same & (lax.rem(row, 32) == other), 0.25, 0.0
    )
    row, column = iota((72, 128), 0), iota((72, 128), 1)
    centre = 1 + column // 2
    other = centre - 1 + 2 * lax.rem(column, 2)
    along_z = jnp.where(row == centre, 0.75, 0.0) + jnp.where(row == other, 0.25, 0.0)
    cells = [coarse[:, x, 0, :] for x in range(4)]
    for x in range(4):
        centre, other = (1, 0, 1, 2, 2, 1, 2, 3)[2 * x : 2 * x + 2]
        mixed = 0.75 * cells[centre] + 0.25 * cells[other]
        wide = jnp.dot(mixed, along_y, precision=HIGHEST, preferred_element_type=F32)
        full = lax.dot_general(
            wide, along_z, (((0,), (0,)), ((), ())), precision=HIGHEST, preferred_element_type=F32
        )
        eddy[:, x] = full.reshape(4, 32, 128)
    copy.wait()


def per_device(state, visc, lift, bias, gains, query, key, value, out, up, down, head):
    hbm = pl.BlockSpec(memory_space=pl.ANY)
    vmem = pltpu.VMEM
    block = (4, 4, 32, 128)
    weights = (lift, bias.reshape(1, 128), gains, query, key, value, out, up, down, head)
    state_next, coarse = pl.pallas_call(
        main_kernel,
        out_shape=(
            jax.ShapeDtypeStruct(block, F32),
            jax.ShapeDtypeStruct((72, 4, 1, 128), F32),
        ),
        in_specs=[hbm] * 12,
        out_specs=(hbm, hbm),
        scratch_shapes=[vmem(block, F32)] * 5
        + [
            vmem((3, 4, 128, 128), F32),
            vmem((3, 4, 128, 128), F32),
            vmem((4, 128, 128), F32),
            vmem((4, 2, 4, 32, 128), BF16),
            vmem((4, 2, 4, 32, 128), BF16),
            vmem((4, 2, 16, 128), F32),
            vmem((4, 2, 16, 128), F32),
            vmem((4, 32, 128), F32),
            vmem((4, 2, 32, 128), F32),
            vmem((2, 256, 128), F32),
            vmem((64, 2, 128), F32),
            vmem((64, 2, 128), F32),
            vmem((16, 2, 2, 32, 128), F32),
            vmem((66, 1, 128), F32),
            vmem((72, 4, 1, 128), F32),
        ]
        + [vmem(w.shape, w.dtype) for w in weights]
        + [
            DMA((2, 4)),
            DMA((10,)),
            DMA((4, 5)),
            DMA((4, 5)),
            DMA,
            DMA,
            DMA,
            DMA,
            DMA,
            DMA((5,)),
        ],
        compiler_params=pltpu.CompilerParams(
            collective_id=0, has_side_effects=True, vmem_limit_bytes=48 << 20
        ),
        name="flow_and_columns",
    )(state, visc, *weights)
    return pl.pallas_call(
        refine_kernel,
        out_shape=(jax.ShapeDtypeStruct(block, F32), jax.ShapeDtypeStruct(block, F32)),
        in_specs=[hbm, pl.BlockSpec(memory_space=pltpu.VMEM)],
        out_specs=(hbm, pl.BlockSpec(memory_space=pltpu.VMEM)),
        scratch_shapes=[DMA],
        name="refine",
    )(state_next, coarse)


def solution(mesh):
    cells = P(None, "gx", "gy", "gz")
    return jax.shard_map(
        per_device,
        mesh=mesh,
        in_specs=(cells, cells) + (P(),) * 10,
        out_specs=(cells, cells),
        check_vma=False,
    )
```

```python
import functools
import math

import jax
import jax.numpy as jnp
from jax import lax
from jax.experimental import pallas as pl
from jax.experimental.pallas import tpu as pltpu
from jax.sharding import PartitionSpec as P

EPSILON = 1e-06
TIME_STEP = 0.3
MESH = pl.DeviceIdType.MESH
F32 = jnp.float32
BF16 = jnp.bfloat16
DMA = pltpu.SemaphoreType.DMA
HIGHEST = lax.Precision.HIGHEST


def iota(shape, dim):
    return lax.broadcasted_iota(jnp.int32, shape, dim)


def rms(values, gain):
    square = jnp.mean(values * values, axis=-1, keepdims=True)
    return values * lax.rsqrt(square + EPSILON) * gain


def gelu(values):
    inner = math.sqrt(2.0 / math.pi) * (values + 0.044715 * (values * values * values))
    return 0.5 * values * (1.0 + jnp.tanh(inner))


def dot(left, right):
    return jnp.dot(left, right, preferred_element_type=F32)


def dot_nt(left, right, precision=None):
    return lax.dot_general(
        left, right, (((1,), (1,)), ((), ())), precision=precision, preferred_element_type=F32
    )


def order4(step):
    return lax.rem(2 + 3 * step + 3 * (step // 2) + 2 * (step // 3), 4)


def peer(step, gx, gy):
    tz = lax.rem(gx // 16 + 1 + step // 32, 2)
    tx = lax.rem(lax.rem(gx // 4, 4) + order4(lax.rem(step // 8, 4)), 4)
    ty = lax.rem(lax.rem(gx, 4) + order4(lax.rem(step // 2, 4)), 4)
    tc = lax.rem(gy + 1 + lax.rem(step, 2), 2)
    return tz * 16 + tx * 4 + ty, tc


def mixer(flat, mask, gains, weights):
    width = flat.shape[1]
    pieces = [slice(g * 128, g * 128 + 128) for g in range(flat.shape[0] // 128)]
    query, key, value, out, up, down = weights
    normed = rms(flat, gains[0]).astype(BF16)
    projected = dot(normed, jnp.concatenate([query, key, value], axis=1)).astype(BF16)
    queries = projected[:, :width]
    keys = projected[:, width : 2 * width]
    values = projected[:, 2 * width :]
    ones = jnp.ones((128, width), BF16)
    scores = [
        jnp.where(mask, dot_nt(queries[p], keys[p]), -1e30) * (width**-0.5) for p in pieces
    ]
    exponent = [jnp.exp(s - jnp.max(s, axis=-1, keepdims=True)).astype(BF16) for s in scores]
    summed = [
        dot(e, jnp.concatenate([values[p], ones], axis=1)) for e, p in zip(exponent, pieces)
    ]
    attended = jnp.concatenate(
        [(s[:, :width] * (1.0 / s[:, width:])).astype(BF16) for s in summed], axis=0
    )
    residual = flat + dot(attended, out)
    again = rms(residual, gains[1]).astype(BF16)
    hidden = gelu(dot(again, up)).astype(BF16)
    return (residual + dot(hidden, down)).astype(BF16)


def main_kernel(
    state_hbm, visc_hbm, lift_hbm, bias_hbm, gains_hbm, query_hbm, key_hbm, value_hbm, out_hbm,
    up_hbm, down_hbm, head_hbm,
    next_hbm, coarse_hbm,
    s0, s1, s2, s3, visc, nu_f, nu_b, nu_sum, xs, xr, ys, yr, zs, zr, pool, filt, recv, hid, cbuf,
    ebuf, lift_w, bias_w, gains_w, query_w, key_w, value_w, out_w, up_w, down_w, head_w,
    load_sem, weight_sem, face_send, face_recv, a_send, a_recv, b_send, b_recv, edge_send, out_sem,
):
    gx, gy, gz = lax.axis_index("gx"), lax.axis_index("gy"), lax.axis_index("gz")
    plane = gx * 2 + gy
    loads = []
    for x in range(4):
        for n, (src, dst) in enumerate(((state_hbm, s0), (visc_hbm, visc))):
            loads.append(pltpu.make_async_copy(src.at[:, x], dst.at[x], load_sem.at[n, x]))
            loads[-1].start()
    weight_pairs = (
        (lift_hbm, lift_w), (bias_hbm, bias_w), (gains_hbm, gains_w), (query_hbm, query_w),
        (key_hbm, key_w), (value_hbm, value_w), (out_hbm, out_w), (up_hbm, up_w),
        (down_hbm, down_w), (head_hbm, head_w),
    )
    weight_loads = []
    for n, (src, dst) in enumerate(weight_pairs):
        weight_loads.append(pltpu.make_async_copy(src, dst, weight_sem.at[n]))
        weight_loads[-1].start()

    barrier = pltpu.get_barrier_semaphore()

    def greet(step, carry):
        tx, ty = peer(step, gx, gy)
        pl.semaphore_signal(barrier, inc=1, device_id={"gx": tx, "gy": ty}, device_id_type=MESH)
        return carry

    z_next, z_last = lax.rem(gz + 1, 4), lax.rem(gz + 3, 4)
    lax.fori_loop(0, 63, greet, 0)
    for target in (z_next, z_last):
        pl.semaphore_signal(barrier, inc=1, device_id={"gz": target}, device_id_type=MESH)
    pl.semaphore_signal(
        barrier, inc=1, device_id={"gx": 0, "gy": 0, "gz": z_next}, device_id_type=MESH
    )
    pl.semaphore_signal(
        barrier, inc=1, device_id={"gx": 31, "gy": 1, "gz": z_last}, device_id_type=MESH
    )

    for copy in loads:
        copy.wait()

    lanes32 = iota((32, 128), 1)

    def stage(e, source):
        xs[e, 0] = source[0].astype(BF16)
        xs[e, 1] = source[3].astype(BF16)
        packed = jnp.zeros((32, 128), F32)
        for x in range(4):
            for f in range(4):
                j = x * 4 + f
                ys[e, 0, j : j + 1, :] = source[x, f, 0:1, :]
                ys[e, 1, j : j + 1, :] = source[x, f, 31:32, :]
                block = source[x, f]
                packed = jnp.where(lanes32 == j, block[:, 0:1], packed)
                packed = jnp.where(lanes32 == 16 + j, block[:, 127:128], packed)
        zs[e] = packed

    x_next, x_last = lax.rem(gx + 1, 32), lax.rem(gx + 31, 32)

    def face_copies(e):
        pairs = (
            (xs.at[e, 1], xr.at[e, 0], {"gx": x_next}),
            (xs.at[e, 0], xr.at[e, 1], {"gx": x_last}),
            (zs.at[e], zr.at[e, 0], {"gz": z_next}),
            (zs.at[e], zr.at[e, 1], {"gz": z_last}),
            (ys.at[e], yr.at[e], {"gy": 1 - gy}),
        )
        return [
            pltpu.make_async_remote_copy(
                src_ref=src, dst_ref=dst, send_sem=face_send.at[e, n], recv_sem=face_recv.at[e, n],
                device_id=device, device_id_type=MESH,
            )
            for n, (src, dst, device) in enumerate(pairs)
        ]

    stage(0, s0)
    stage(1, visc)
    extra = jnp.where(plane == 0, 64, 0) + jnp.where(plane == 63, 64, 0)
    pl.semaphore_wait(barrier, 65 + extra)
    copies = [face_copies(e) for e in range(4)]
    for e in range(2):
        for copy in copies[e]:
            copy.start()

    rows = iota((128, 128), 0)
    lanes = iota((128, 128), 1)
    row32 = lax.rem(rows, 32)

    def neighbours(e, source, x):
        middle = source[x].reshape(128, 128)
        if x == 0:
            x_b = xr[e, 0].astype(F32).reshape(128, 128)
        else:
            x_b = source[x - 1].reshape(128, 128)
        if x == 3:
            x_f = xr[e, 1].astype(F32).reshape(128, 128)
        else:
            x_f = source[x + 1].reshape(128, 128)

        def spread(side):
            return jnp.concatenate(
                [
                    jnp.broadcast_to(yr[e, side, x * 4 + f : x * 4 + f + 1, :], (32, 128))
                    for f in range(4)
                ],
                axis=0,
            )

        y_b = jnp.where(row32 == 0, spread(1), pltpu.roll(middle, 1, 0))
        y_f = jnp.where(row32 == 31, spread(0), pltpu.roll(middle, 127, 0))

        def column(side, first):
            return jnp.concatenate(
                [
                    jnp.broadcast_to(
                        zr[e, side, :, first + x * 4 + f : first + x * 4 + f + 1], (32, 128)
                    )
                    for f in range(4)
                ],
                axis=0,
            )

        z_b = jnp.where(lanes == 0, column(0, 16), pltpu.roll(middle, 1, 1))
        z_f = jnp.where(lanes == 127, column(1, 0), pltpu.roll(middle, 127, 1))
        return middle, ((x_b, x_f), (y_b, y_f), (z_b, z_f))

    def advance(e, source, combine):
        for x in range(4):
            middle, pairs = neighbours(e, source, x)
            total = -middle * nu_sum[x]
            for d, (before, after) in enumerate(pairs):
                half = (0.5 * TIME_STEP) * source[x, d]
                half = jnp.concatenate([half] * 4, axis=0)
                total += after * (nu_f[d, x] - half) + before * (nu_b[d, x] + half)
            combine(x, middle + total)

    for copy in copies[1]:
        copy.wait_recv()
    for x in range(4):
        middle, pairs = neighbours(1, visc, x)
        total = jnp.zeros((128, 128), F32)
        for d, (before, after) in enumerate(pairs):
            forward = (0.5 * TIME_STEP) * (middle + after)
            backward = (0.5 * TIME_STEP) * (middle + before)
            nu_f[d, x] = forward
            nu_b[d, x] = backward
            total += forward + backward
        nu_sum[x] = total

    def first(x, value):
        s1[x] = value.reshape(4, 32, 128)

    def second(x, value):
        s2[x] = (0.75 * s0[x].reshape(128, 128) + 0.25 * value).reshape(4, 32, 128)

    def third(x, value):
        s3[x] = (s0[x].reshape(128, 128) / 3.0 + (2.0 / 3.0) * value).reshape(4, 32, 128)

    for copy in copies[0]:
        copy.wait_recv()
    advance(0, s0, first)
    stage(2, s1)
    for copy in copies[2]:
        copy.start()
    for copy in copies[2]:
        copy.wait_recv()
    advance(2, s1, second)
    stage(3, s2)
    for copy in copies[3]:
        copy.start()
    for copy in copies[3]:
        copy.wait_recv()
    advance(3, s2, third)

    results = []
    for x in range(4):
        results.append(pltpu.make_async_copy(s3.at[x], next_hbm.at[:, x], out_sem.at[x]))
        results[-1].start()

    pick = jnp.where(iota((64, 128), 1) // 2 == iota((64, 128), 0), 0.125, 0.0)
    for x in range(2):
        one, two = s3[2 * x].reshape(128, 128), s3[2 * x + 1].reshape(128, 128)
        pool[x, 0:128] = one + two
        pool[x, 128:256] = one * one + two * two
        paired = pool[x, pl.ds(0, 128, stride=2), :] + pool[x, pl.ds(1, 128, stride=2), :]
        filt[:, x, :] = dot_nt(pick, paired, HIGHEST)

    slot = (gx // 4) * 8 + gy * 4 + lax.rem(gx, 4)

    def send_filtered(step, carry):
        tx, ty = peer(step, gx, gy)
        pltpu.make_async_remote_copy(
            src_ref=filt.at[tx * 2 + ty], dst_ref=recv.at[slot], send_sem=a_send,
            recv_sem=a_recv, device_id={"gx": tx, "gy": ty}, device_id_type=MESH,
        ).start()
        return carry

    lax.fori_loop(0, 63, send_filtered, 0)
    recv[pl.ds(slot, 1)] = filt[pl.ds(plane, 1)]

    for copy in weight_loads:
        copy.wait()
    lift_rows = jnp.concatenate(
        [jnp.broadcast_to(lift_w[c : c + 1, :], (16, 128)) for c in range(8)], axis=0
    )
    head_all = head_w[...].astype(F32)
    head_rows = jnp.concatenate(
        [jnp.broadcast_to(head_all[f : f + 1, :], (32, 128)) for f in range(4)], axis=0
    ).astype(BF16)

    a_all = pltpu.make_async_remote_copy(
        src_ref=filt.at[pl.ds(0, 63)], dst_ref=recv.at[pl.ds(0, 63)], send_sem=a_send,
        recv_sem=a_recv, device_id={"gy": 1 - gy}, device_id_type=MESH,
    )
    a_all.wait_recv()

    filtered = jnp.concatenate([recv[:, 0, :], recv[:, 1, :]], axis=0)
    lane16 = lax.rem(lanes, 16)

    def block_weights(i):
        return (query_w[i], key_w[i], value_w[i], out_w[i], up_w[i], down_w[i])

    def gain(i):
        return gains_w[i : i + 1, :]

    inputs = jnp.concatenate(
        [jnp.where(lane16 == y, filtered, 0.0) for y in range(16)], axis=0
    )
    lifted = (
        jnp.dot(inputs, lift_rows, precision=HIGHEST, preferred_element_type=F32) + bias_w[...]
    )
    features = gelu(rms(lifted, gain(0))).astype(BF16).astype(F32)
    along_x = lax.rem(rows // 4, 2) == lax.rem(lanes // 4, 2)
    result = mixer(features, along_x, (gain(1), gain(2)), block_weights(0))
    for y in range(16):
        part = result[y * 128 : y * 128 + 128].astype(F32)
        for c in range(16):
            hid[c, y] = part[c * 8 : c * 8 + 8]

    along_y = lax.rem(rows, 4) == lax.rem(lanes, 4)
    result = mixer(
        hid[...].reshape(2048, 128), along_y, (gain(3), gain(4)), block_weights(1)
    )
    final = rms(result.astype(F32), gain(5)).astype(BF16)
    spread = dot_nt(final, head_rows)
    own_lane = lax.rem(lanes, 32) == lax.rem(rows // 4, 2) * 16 + rows // 8
    for c in range(16):
        part = jnp.where(own_lane, spread[c * 128 : c * 128 + 128], 0.0).reshape(16, 8, 128)
        part = jnp.sum(part, axis=0)
        logits = part + pltpu.roll(part, 4, 0)
        coefficient = 0.05 + 0.45 * (1.0 / (1.0 + jnp.exp(-logits)))
        for r in range(4):
            cbuf[1 + c // 8 + 2 * (4 * (c % 8) + r)] = coefficient[r : r + 1, :]
    cbuf[0] = cbuf[64]
    cbuf[65] = cbuf[1]

    def send_coarse(step, carry):
        tx, ty = peer(step, gx, gy)
        pltpu.make_async_remote_copy(
            src_ref=cbuf.at[pl.ds(2 * tx, 4)], dst_ref=ebuf.at[plane + 1], send_sem=b_send,
            recv_sem=b_recv, device_id={"gx": tx, "gy": ty}, device_id_type=MESH,
        ).start()
        return carry

    def send_edge(slot, target_z, step, carry):
        tx, ty = peer(step, gx, gy)
        pltpu.make_async_remote_copy(
            src_ref=cbuf.at[pl.ds(2 * tx, 4)], dst_ref=ebuf.at[slot], send_sem=edge_send,
            recv_sem=b_recv, device_id={"gx": tx, "gy": ty, "gz": target_z}, device_id_type=MESH,
        ).start()
        return carry

    @pl.when(plane == 63)
    def _():
        lax.fori_loop(0, 64, functools.partial(send_edge, 0, z_next), 0)

    @pl.when(plane == 0)
    def _():
        lax.fori_loop(0, 64, functools.partial(send_edge, 65, z_last), 0)

    lax.fori_loop(0, 63, send_coarse, 0)
    ebuf[pl.ds(plane + 1, 1)] = cbuf[pl.ds(2 * gx, 4)].reshape(1, 4, 1, 128)
    ebuf[66:72] = jnp.zeros((6, 4, 1, 128), F32)
    b_all = pltpu.make_async_remote_copy(
        src_ref=ebuf.at[pl.ds(0, 63)], dst_ref=ebuf.at[pl.ds(0, 65)], send_sem=b_send,
        recv_sem=b_recv, device_id={"gy": 1 - gy}, device_id_type=MESH,
    )
    b_all.wait_recv()
    final_copy = pltpu.make_async_copy(ebuf, coarse_hbm, out_sem.at[4])
    final_copy.start()
    for e in range(4):
        for copy in copies[e]:
            copy.wait_send()
    a_all.wait_send()
    b_all.wait_send()

    @pl.when((plane == 63) | (plane == 0))
    def _():
        pltpu.make_async_remote_copy(
            src_ref=ebuf.at[pl.ds(0, 64)], dst_ref=ebuf.at[pl.ds(0, 64)], send_sem=edge_send,
            recv_sem=b_recv, device_id={"gy": 1 - gy}, device_id_type=MESH,
        ).wait_send()

    for copy in results:
        copy.wait()
    final_copy.wait()


def refine_kernel(next_hbm, coarse_hbm, next_out, eddy_hbm, coarse, passed, eddy, sem):
    load = pltpu.make_async_copy(coarse_hbm, coarse, sem.at[0])
    load.start()
    first = pltpu.make_async_copy(next_hbm, passed, sem.at[1])
    first.start()
    gy = lax.axis_index("gy")
    row, column = iota((128, 128), 0), iota((128, 128), 1)
    fine = lax.rem(column, 32)
    centre = gy * 16 + fine // 2
    other = lax.rem(centre + 31 + 2 * lax.rem(fine, 2), 32)
    same = row // 32 == column // 32
    along_y = jnp.where(same & (lax.rem(row, 32) == centre), 0.75, 0.0) + jnp.where(
        same & (lax.rem(row, 32) == other), 0.25, 0.0
    )
    row, column = iota((72, 128), 0), iota((72, 128), 1)
    centre = 1 + column // 2
    other = centre - 1 + 2 * lax.rem(column, 2)
    along_z = jnp.where(row == centre, 0.75, 0.0) + jnp.where(row == other, 0.25, 0.0)
    load.wait()
    cells = [coarse[:, x, 0, :] for x in range(4)]
    results = []
    for x in range(4):
        centre, other = (1, 0, 1, 2, 2, 1, 2, 3)[2 * x : 2 * x + 2]
        mixed = 0.75 * cells[centre] + 0.25 * cells[other]
        wide = jnp.dot(mixed, along_y, precision=HIGHEST, preferred_element_type=F32)
        full = lax.dot_general(
            wide, along_z, (((0,), (0,)), ((), ())), precision=HIGHEST, preferred_element_type=F32
        )
        eddy[x] = full.reshape(4, 32, 128)
        results.append(pltpu.make_async_copy(eddy.at[x], eddy_hbm.at[:, x], sem.at[3 + x]))
        results[-1].start()
        if x == 0:
            first.wait()
            results.append(pltpu.make_async_copy(passed, next_out, sem.at[2]))
            results[-1].start()
    for copy in results:
        copy.wait()


def per_device(state, visc, lift, bias, gains, query, key, value, out, up, down, head):
    hbm = pl.BlockSpec(memory_space=pl.ANY)
    vmem = pltpu.VMEM
    block = (4, 4, 32, 128)
    weights = (lift, bias.reshape(1, 128), gains, query, key, value, out, up, down, head.T)
    state_next, coarse = pl.pallas_call(
        main_kernel,
        out_shape=(
            jax.ShapeDtypeStruct(block, F32),
            jax.ShapeDtypeStruct((72, 4, 1, 128), F32),
        ),
        in_specs=[hbm] * 12,
        out_specs=(hbm, hbm),
        scratch_shapes=[vmem(block, F32)] * 5
        + [
            vmem((3, 4, 128, 128), F32),
            vmem((3, 4, 128, 128), F32),
            vmem((4, 128, 128), F32),
            vmem((4, 2, 4, 32, 128), BF16),
            vmem((4, 2, 4, 32, 128), BF16),
            vmem((4, 2, 16, 128), F32),
            vmem((4, 2, 16, 128), F32),
            vmem((4, 32, 128), F32),
            vmem((4, 2, 32, 128), F32),
            vmem((2, 256, 128), F32),
            vmem((64, 2, 128), F32),
            vmem((64, 2, 128), F32),
            vmem((16, 16, 8, 128), F32),
            vmem((66, 1, 128), F32),
            vmem((72, 4, 1, 128), F32),
        ]
        + [vmem(w.shape, w.dtype) for w in weights]
        + [
            DMA((2, 4)),
            DMA((10,)),
            DMA((4, 5)),
            DMA((4, 5)),
            DMA,
            DMA,
            DMA,
            DMA,
            DMA,
            DMA((5,)),
        ],
        compiler_params=pltpu.CompilerParams(
            collective_id=0, has_side_effects=True, vmem_limit_bytes=60 << 20
        ),
        name="flow_and_columns",
    )(state, visc, *weights)
    return pl.pallas_call(
        refine_kernel,
        out_shape=(jax.ShapeDtypeStruct(block, F32), jax.ShapeDtypeStruct(block, F32)),
        in_specs=[hbm, hbm],
        out_specs=(hbm, hbm),
        scratch_shapes=[
            vmem((72, 4, 1, 128), F32),
            vmem(block, F32),
            vmem(block, F32),
            DMA((7,)),
        ],
        compiler_params=pltpu.CompilerParams(vmem_limit_bytes=60 << 20),
        name="refine",
    )(state_next, coarse)


def solution(mesh):
    cells = P(None, "gx", "gy", "gz")
    return jax.shard_map(
        per_device,
        mesh=mesh,
        in_specs=(cells, cells) + (P(),) * 10,
        out_specs=(cells, cells),
        check_vma=False,
    )
```

```python
import math

import jax
import jax.numpy as jnp
from jax import lax
from jax.experimental import pallas as pl
from jax.experimental.pallas import tpu as pltpu
from jax.sharding import PartitionSpec as P

EPSILON = 1e-06
TIME_STEP = 0.3
MESH = pl.DeviceIdType.MESH
F32 = jnp.float32
BF16 = jnp.bfloat16
DMA = pltpu.SemaphoreType.DMA
HIGHEST = lax.Precision.HIGHEST


def iota(shape, dim):
    return lax.broadcasted_iota(jnp.int32, shape, dim)


def rms(values, gain):
    square = jnp.mean(values * values, axis=-1, keepdims=True)
    return values * lax.rsqrt(square + EPSILON) * gain


def gelu(values):
    inner = math.sqrt(2.0 / math.pi) * (values + 0.044715 * (values * values * values))
    return 0.5 * values * (1.0 + jnp.tanh(inner))


def dot(left, right):
    return jnp.dot(left, right, preferred_element_type=F32)


def dot_nt(left, right, precision=None):
    return lax.dot_general(
        left, right, (((1,), (1,)), ((), ())), precision=precision, preferred_element_type=F32
    )


def peers(gx, gy):
    z, x, y = gx // 16, lax.rem(gx // 4, 4), lax.rem(gx, 4)

    def ring(place):
        return [lax.rem(place + 2, 4), lax.rem(place + 1, 4), lax.rem(place + 3, 4), place]

    found = [
        (tz * 16 + tx * 4 + ty, tc)
        for tz in (1 - z, z)
        for tx in ring(x)
        for ty in ring(y)
        for tc in (1 - gy, gy)
    ]
    return found[:63]


def mixer(flat, mask, gains, weights):
    width = flat.shape[1]
    pieces = [slice(g * 128, g * 128 + 128) for g in range(flat.shape[0] // 128)]
    query, key, value, out, up, down = weights
    normed = rms(flat, gains[0]).astype(BF16)
    projected = dot(normed, jnp.concatenate([query, key, value], axis=1)).astype(BF16)
    queries = projected[:, :width]
    keys = projected[:, width : 2 * width]
    values = projected[:, 2 * width :]
    ones = jnp.ones((128, width), BF16)
    scores = [
        jnp.where(mask, dot_nt(queries[p], keys[p]), -1e30) * (width**-0.5) for p in pieces
    ]
    exponent = [jnp.exp(s - jnp.max(s, axis=-1, keepdims=True)).astype(BF16) for s in scores]
    summed = [
        dot(e, jnp.concatenate([values[p], ones], axis=1)) for e, p in zip(exponent, pieces)
    ]
    attended = jnp.concatenate(
        [(s[:, :width] * (1.0 / s[:, width:])).astype(BF16) for s in summed], axis=0
    )
    residual = flat + dot(attended, out)
    again = rms(residual, gains[1]).astype(BF16)
    hidden = gelu(dot(again, up)).astype(BF16)
    return (residual + dot(hidden, down)).astype(BF16)


def main_kernel(
    state_hbm, visc_hbm, lift_hbm, bias_hbm, gains_hbm, query_hbm, key_hbm, value_hbm, out_hbm,
    up_hbm, down_hbm, head_hbm,
    s3, eddy,
    s0, s1, s2, visc, nu_f, nu_b, nu_sum, xs, xr, ys, yr, zs, zr, pool, filt, recv, hid, cbuf,
    ebuf, lift_w, bias_w, gains_w, query_w, key_w, value_w, out_w, up_w, down_w, head_w,
    load_sem, weight_sem, face_send, face_recv, a_send, a_recv, b_send, b_recv, edge_send,
):
    gx, gy, gz = lax.axis_index("gx"), lax.axis_index("gy"), lax.axis_index("gz")
    plane = gx * 2 + gy
    others = peers(gx, gy)
    loads = []
    for x in (0, 3, 1, 2):
        for n, (src, dst) in enumerate(((state_hbm, s0), (visc_hbm, visc))):
            loads.append(pltpu.make_async_copy(src.at[:, x], dst.at[x], load_sem.at[n, x]))
            loads[-1].start()

    barrier = pltpu.get_barrier_semaphore()
    z_next, z_last = lax.rem(gz + 1, 4), lax.rem(gz + 3, 4)
    for tx, ty in others:
        pl.semaphore_signal(barrier, inc=1, device_id={"gx": tx, "gy": ty}, device_id_type=MESH)
    for target in (z_next, z_last):
        pl.semaphore_signal(barrier, inc=1, device_id={"gz": target}, device_id_type=MESH)
    pl.semaphore_signal(
        barrier, inc=1, device_id={"gx": 0, "gy": 0, "gz": z_next}, device_id_type=MESH
    )
    pl.semaphore_signal(
        barrier, inc=1, device_id={"gx": 31, "gy": 1, "gz": z_last}, device_id_type=MESH
    )
    weight_pairs = (
        (lift_hbm, lift_w), (bias_hbm, bias_w), (gains_hbm, gains_w), (query_hbm, query_w),
        (key_hbm, key_w), (value_hbm, value_w), (out_hbm, out_w), (up_hbm, up_w),
        (down_hbm, down_w), (head_hbm, head_w),
    )
    weight_loads = []
    for n, (src, dst) in enumerate(weight_pairs):
        weight_loads.append(pltpu.make_async_copy(src, dst, weight_sem.at[n]))
        weight_loads[-1].start()

    for copy in loads:
        copy.wait()

    lanes32 = iota((32, 128), 1)

    def stage_x(e, source):
        xs[e, 0] = source[0].astype(BF16)
        xs[e, 1] = source[3].astype(BF16)

    def stage_yz(e, source):
        packed = jnp.zeros((32, 128), F32)
        for x in range(4):
            for f in range(4):
                j = x * 4 + f
                ys[e, 0, j : j + 1, :] = source[x, f, 0:1, :]
                ys[e, 1, j : j + 1, :] = source[x, f, 31:32, :]
                block = source[x, f]
                packed = jnp.where(lanes32 == j, block[:, 0:1], packed)
                packed = jnp.where(lanes32 == 16 + j, block[:, 127:128], packed)
        zs[e] = packed

    x_next, x_last = lax.rem(gx + 1, 32), lax.rem(gx + 31, 32)

    def face_copies(e):
        pairs = (
            (xs.at[e, 1], xr.at[e, 0], {"gx": x_next}),
            (xs.at[e, 0], xr.at[e, 1], {"gx": x_last}),
            (zs.at[e], zr.at[e, 0], {"gz": z_next}),
            (zs.at[e], zr.at[e, 1], {"gz": z_last}),
            (ys.at[e], yr.at[e], {"gy": 1 - gy}),
        )
        return [
            pltpu.make_async_remote_copy(
                src_ref=src, dst_ref=dst, send_sem=face_send.at[e, n], recv_sem=face_recv.at[e, n],
                device_id=device, device_id_type=MESH,
            )
            for n, (src, dst, device) in enumerate(pairs)
        ]

    copies = [face_copies(e) for e in range(4)]

    def start_x(e):
        copies[e][0].start()
        copies[e][1].start()

    def start_yz(e):
        for copy in copies[e][2:]:
            copy.start()

    def wait_x(e):
        copies[e][0].wait_recv()
        copies[e][1].wait_recv()

    def wait_yz(e):
        for copy in copies[e][2:]:
            copy.wait_recv()

    stage_x(1, visc)
    stage_x(0, s0)
    extra = jnp.where(plane == 0, 64, 0) + jnp.where(plane == 63, 64, 0)
    pl.semaphore_wait(barrier, 65 + extra)
    for e, source in ((1, visc), (0, s0)):
        start_x(e)
    for e, source in ((1, visc), (0, s0)):
        stage_yz(e, source)
        start_yz(e)

    rows = iota((128, 128), 0)
    lanes = iota((128, 128), 1)
    row32 = lax.rem(rows, 32)

    def neighbours(e, source, x):
        middle = source[x].reshape(128, 128)
        if x == 0:
            x_b = xr[e, 0].astype(F32).reshape(128, 128)
        else:
            x_b = source[x - 1].reshape(128, 128)
        if x == 3:
            x_f = xr[e, 1].astype(F32).reshape(128, 128)
        else:
            x_f = source[x + 1].reshape(128, 128)

        def spread(side):
            return jnp.concatenate(
                [
                    jnp.broadcast_to(yr[e, side, x * 4 + f : x * 4 + f + 1, :], (32, 128))
                    for f in range(4)
                ],
                axis=0,
            )

        y_b = jnp.where(row32 == 0, spread(1), pltpu.roll(middle, 1, 0))
        y_f = jnp.where(row32 == 31, spread(0), pltpu.roll(middle, 127, 0))

        def column(side, first):
            return jnp.concatenate(
                [
                    jnp.broadcast_to(
                        zr[e, side, :, first + x * 4 + f : first + x * 4 + f + 1], (32, 128)
                    )
                    for f in range(4)
                ],
                axis=0,
            )

        z_b = jnp.where(lanes == 0, column(0, 16), pltpu.roll(middle, 1, 1))
        z_f = jnp.where(lanes == 127, column(1, 0), pltpu.roll(middle, 127, 1))
        return middle, ((x_b, x_f), (y_b, y_f), (z_b, z_f))

    def advance(e, source, combine, planes):
        for x in planes:
            middle, pairs = neighbours(e, source, x)
            total = -middle * nu_sum[x]
            for d, (before, after) in enumerate(pairs):
                half = (0.5 * TIME_STEP) * source[x, d]
                half = jnp.concatenate([half] * 4, axis=0)
                total += after * (nu_f[d, x] - half) + before * (nu_b[d, x] + half)
            combine(x, middle + total)

    def mean_viscosity(planes):
        for x in planes:
            middle, pairs = neighbours(1, visc, x)
            total = jnp.zeros((128, 128), F32)
            for d, (before, after) in enumerate(pairs):
                forward = (0.5 * TIME_STEP) * (middle + after)
                backward = (0.5 * TIME_STEP) * (middle + before)
                nu_f[d, x] = forward
                nu_b[d, x] = backward
                total += forward + backward
            nu_sum[x] = total

    def first(x, value):
        s1[x] = value.reshape(4, 32, 128)

    def second(x, value):
        s2[x] = (0.75 * s0[x].reshape(128, 128) + 0.25 * value).reshape(4, 32, 128)

    def third(x, value):
        s3[:, x] = (s0[x].reshape(128, 128) / 3.0 + (2.0 / 3.0) * value).reshape(4, 32, 128)

    wait_yz(1)
    mean_viscosity((1, 2))
    wait_yz(0)
    advance(0, s0, first, (1, 2))
    wait_x(1)
    mean_viscosity((0, 3))
    wait_x(0)
    advance(0, s0, first, (0, 3))
    for e, source, target, combine in ((2, s1, s2, second), (3, s2, s3, third)):
        stage_x(e, source)
        start_x(e)
        stage_yz(e, source)
        start_yz(e)
        wait_yz(e)
        advance(e, source, combine, (1, 2))
        wait_x(e)
        advance(e, source, combine, (0, 3))

    pick = jnp.where(iota((64, 128), 1) // 2 == iota((64, 128), 0), 0.125, 0.0)
    for x in range(2):
        one, two = (s3[:, 2 * x + i].reshape(128, 128) for i in range(2))
        pool[x, 0:128] = one + two
        pool[x, 128:256] = one * one + two * two
        paired = pool[x, pl.ds(0, 128, stride=2), :] + pool[x, pl.ds(1, 128, stride=2), :]
        filt[:, x, :] = dot_nt(pick, paired, HIGHEST)

    slot = (gx // 4) * 8 + gy * 4 + lax.rem(gx, 4)

    for tx, ty in others:
        pltpu.make_async_remote_copy(
            src_ref=filt.at[tx * 2 + ty], dst_ref=recv.at[slot], send_sem=a_send,
            recv_sem=a_recv, device_id={"gx": tx, "gy": ty}, device_id_type=MESH,
        ).start()
    recv[pl.ds(slot, 1)] = filt[pl.ds(plane, 1)]

    for copy in weight_loads:
        copy.wait()
    lift_rows = jnp.concatenate(
        [jnp.broadcast_to(lift_w[c : c + 1, :], (16, 128)) for c in range(8)], axis=0
    )
    head_all = head_w[...].astype(F32)
    head_rows = jnp.concatenate(
        [jnp.broadcast_to(head_all[f : f + 1, :], (32, 128)) for f in range(4)], axis=0
    ).astype(BF16)

    a_all = pltpu.make_async_remote_copy(
        src_ref=filt.at[pl.ds(0, 63)], dst_ref=recv.at[pl.ds(0, 63)], send_sem=a_send,
        recv_sem=a_recv, device_id={"gy": 1 - gy}, device_id_type=MESH,
    )
    a_all.wait_recv()

    filtered = jnp.concatenate([recv[:, 0, :], recv[:, 1, :]], axis=0)
    lane16 = lax.rem(lanes, 16)

    def block_weights(i):
        return (query_w[i], key_w[i], value_w[i], out_w[i], up_w[i], down_w[i])

    def gain(i):
        return gains_w[i : i + 1, :]

    inputs = jnp.concatenate(
        [jnp.where(lane16 == y, filtered, 0.0) for y in range(16)], axis=0
    )
    lifted = (
        jnp.dot(inputs, lift_rows, precision=HIGHEST, preferred_element_type=F32) + bias_w[...]
    )
    features = gelu(rms(lifted, gain(0))).astype(BF16).astype(F32)
    along_x = lax.rem(rows // 4, 2) == lax.rem(lanes // 4, 2)
    result = mixer(features, along_x, (gain(1), gain(2)), block_weights(0))
    for y in range(16):
        part = result[y * 128 : y * 128 + 128].astype(F32)
        for c in range(16):
            hid[c, y] = part[c * 8 : c * 8 + 8]

    along_y = lax.rem(rows, 4) == lax.rem(lanes, 4)
    result = mixer(
        hid[...].reshape(2048, 128), along_y, (gain(3), gain(4)), block_weights(1)
    )
    final = rms(result.astype(F32), gain(5)).astype(BF16)
    spread = dot_nt(final, head_rows)
    own_lane = lax.rem(lanes, 32) == lax.rem(rows // 4, 2) * 16 + rows // 8
    for c in range(16):
        part = jnp.where(own_lane, spread[c * 128 : c * 128 + 128], 0.0).reshape(16, 8, 128)
        part = jnp.sum(part, axis=0)
        logits = part + pltpu.roll(part, 4, 0)
        coefficient = 0.05 + 0.45 * (1.0 / (1.0 + jnp.exp(-logits)))
        for r in range(4):
            cbuf[1 + c // 8 + 2 * (4 * (c % 8) + r)] = coefficient[r : r + 1, :]
    cbuf[0] = cbuf[64]
    cbuf[65] = cbuf[1]

    def send_edge(slot, target_z, targets):
        for tx, ty in targets:
            pltpu.make_async_remote_copy(
                src_ref=cbuf.at[pl.ds(2 * tx, 4)], dst_ref=ebuf.at[slot], send_sem=edge_send,
                recv_sem=b_recv, device_id={"gx": tx, "gy": ty, "gz": target_z},
                device_id_type=MESH,
            ).start()

    for half in (slice(0, 32), slice(32, 64)):
        for tx, ty in others[half]:
            pltpu.make_async_remote_copy(
                src_ref=cbuf.at[pl.ds(2 * tx, 4)], dst_ref=ebuf.at[plane + 1], send_sem=b_send,
                recv_sem=b_recv, device_id={"gx": tx, "gy": ty}, device_id_type=MESH,
            ).start()

        @pl.when(plane == 63)
        def _(half=half):
            send_edge(0, z_next, (others + [(gx, gy)])[half])

        @pl.when(plane == 0)
        def _(half=half):
            send_edge(65, z_last, (others + [(gx, gy)])[half])

    ebuf[pl.ds(plane + 1, 1)] = cbuf[pl.ds(2 * gx, 4)].reshape(1, 4, 1, 128)
    ebuf[66:72] = jnp.zeros((6, 4, 1, 128), F32)
    b_all = pltpu.make_async_remote_copy(
        src_ref=ebuf.at[pl.ds(0, 63)], dst_ref=ebuf.at[pl.ds(0, 65)], send_sem=b_send,
        recv_sem=b_recv, device_id={"gy": 1 - gy}, device_id_type=MESH,
    )
    row, column = rows, lanes
    fine = lax.rem(column, 32)
    centre = gy * 16 + fine // 2
    other = lax.rem(centre + 31 + 2 * lax.rem(fine, 2), 32)
    same = row // 32 == column // 32
    along_y = jnp.where(same & (lax.rem(row, 32) == centre), 0.75, 0.0) + jnp.where(
        same & (lax.rem(row, 32) == other), 0.25, 0.0
    )
    row, column = iota((72, 128), 0), iota((72, 128), 1)
    centre = 1 + column // 2
    other = centre - 1 + 2 * lax.rem(column, 2)
    along_z = jnp.where(row == centre, 0.75, 0.0) + jnp.where(row == other, 0.25, 0.0)
    b_all.wait_recv()
    cells = [ebuf[:, x, 0, :] for x in range(4)]
    for x in range(4):
        centre, other = (1, 0, 1, 2, 2, 1, 2, 3)[2 * x : 2 * x + 2]
        mixed = 0.75 * cells[centre] + 0.25 * cells[other]
        wide = jnp.dot(mixed, along_y, precision=HIGHEST, preferred_element_type=F32)
        full = lax.dot_general(
            wide, along_z, (((0,), (0,)), ((), ())), precision=HIGHEST, preferred_element_type=F32
        )
        eddy[:, x] = full.reshape(4, 32, 128)
    for e in range(4):
        for copy in copies[e]:
            copy.wait_send()
    a_all.wait_send()
    b_all.wait_send()

    @pl.when((plane == 63) | (plane == 0))
    def _():
        pltpu.make_async_remote_copy(
            src_ref=ebuf.at[pl.ds(0, 64)], dst_ref=ebuf.at[pl.ds(0, 64)], send_sem=edge_send,
            recv_sem=b_recv, device_id={"gy": 1 - gy}, device_id_type=MESH,
        ).wait_send()


def store_kernel(first, second, first_out, second_out, sem):
    copies = [
        pltpu.make_async_copy(first, first_out, sem.at[0]),
        pltpu.make_async_copy(second, second_out, sem.at[1]),
    ]
    for copy in copies:
        copy.start()
    for copy in copies:
        copy.wait()


def per_device(state, visc, lift, bias, gains, query, key, value, out, up, down, head):
    hbm = pl.BlockSpec(memory_space=pl.ANY)
    vmem = pltpu.VMEM
    block = (4, 4, 32, 128)
    weights = (lift, bias.reshape(1, 128), gains, query, key, value, out, up, down, head.T)
    results = pl.pallas_call(
        main_kernel,
        out_shape=(vmem(block, F32), vmem(block, F32)),
        in_specs=[hbm] * 12,
        out_specs=(pl.BlockSpec(memory_space=vmem),) * 2,
        scratch_shapes=[vmem(block, F32)] * 4
        + [
            vmem((3, 4, 128, 128), F32),
            vmem((3, 4, 128, 128), F32),
            vmem((4, 128, 128), F32),
            vmem((4, 2, 4, 32, 128), BF16),
            vmem((4, 2, 4, 32, 128), BF16),
            vmem((4, 2, 16, 128), F32),
            vmem((4, 2, 16, 128), F32),
            vmem((4, 32, 128), F32),
            vmem((4, 2, 32, 128), F32),
            vmem((2, 256, 128), F32),
            vmem((64, 2, 128), F32),
            vmem((64, 2, 128), F32),
            vmem((16, 16, 8, 128), F32),
            vmem((66, 1, 128), F32),
            vmem((72, 4, 1, 128), F32),
        ]
        + [vmem(w.shape, w.dtype) for w in weights]
        + [
            DMA((2, 4)),
            DMA((10,)),
            DMA((4, 5)),
            DMA((4, 5)),
            DMA,
            DMA,
            DMA,
            DMA,
            DMA,
        ],
        compiler_params=pltpu.CompilerParams(
            collective_id=0, has_side_effects=True, vmem_limit_bytes=60 << 20
        ),
        name="flow_and_columns",
    )(state, visc, *weights)
    return pl.pallas_call(
        store_kernel,
        out_shape=(jax.ShapeDtypeStruct(block, F32),) * 2,
        in_specs=[hbm, hbm],
        out_specs=(hbm, hbm),
        scratch_shapes=[DMA((2,))],
        compiler_params=pltpu.CompilerParams(vmem_limit_bytes=1 << 20),
        name="store",
    )(*results)


def solution(mesh):
    cells = P(None, "gx", "gy", "gz")
    return jax.shard_map(
        per_device,
        mesh=mesh,
        in_specs=(cells, cells) + (P(),) * 10,
        out_specs=(cells, cells),
        check_vma=False,
    )
```

```python
import math

import jax
import jax.numpy as jnp
from jax import lax
from jax.experimental import pallas as pl
from jax.experimental.pallas import tpu as pltpu
from jax.sharding import PartitionSpec as P

EPSILON = 1e-06
TIME_STEP = 0.3
MESH = pl.DeviceIdType.MESH
F32 = jnp.float32
BF16 = jnp.bfloat16
DMA = pltpu.SemaphoreType.DMA
HIGHEST = lax.Precision.HIGHEST


def iota(shape, dim):
    return lax.broadcasted_iota(jnp.int32, shape, dim)


def split(values, count):
    parts = []
    for _ in range(count):
        parts.append(values.astype(BF16))
        values = values - parts[-1].astype(F32)
    return parts


def rms(values, gain):
    square = jnp.mean(values * values, axis=-1, keepdims=True)
    return values * lax.rsqrt(square + EPSILON) * gain


def gelu(values):
    inner = math.sqrt(2.0 / math.pi) * (values + 0.044715 * (values * values * values))
    return 0.5 * values * (1.0 + jnp.tanh(inner))


def dot(left, right):
    return jnp.dot(left, right, preferred_element_type=F32)


def dot_nt(left, right, precision=None):
    return lax.dot_general(
        left, right, (((1,), (1,)), ((), ())), precision=precision, preferred_element_type=F32
    )


def peers(gx, gy):
    z, x, y = gx // 16, lax.rem(gx // 4, 4), lax.rem(gx, 4)

    def ring(place):
        return [lax.rem(place + 2, 4), lax.rem(place + 1, 4), lax.rem(place + 3, 4), place]

    found = [
        (tz * 16 + tx * 4 + ty, tc)
        for tz in (1 - z, z)
        for tx in ring(x)
        for ty in ring(y)
        for tc in (1 - gy, gy)
    ]
    return found[:63]


def project(flat, gain, weights):
    query, key, value = weights[:3]
    normed = rms(flat, gain).astype(BF16)
    return dot(normed, jnp.concatenate([query, key, value], axis=1)).astype(BF16)


def mixer(flat, projected, mask, gain, weights):
    width = flat.shape[1]
    pieces = [slice(g * 128, g * 128 + 128) for g in range(flat.shape[0] // 128)]
    out, up, down = weights[3:]
    queries = projected[:, :width]
    keys = projected[:, width : 2 * width]
    values = projected[:, 2 * width :]
    ones = jnp.ones((128, width), BF16)
    scores = [
        jnp.where(mask, dot_nt(queries[p], keys[p]), -1e30) * (width**-0.5) for p in pieces
    ]
    exponent = [jnp.exp(s - jnp.max(s, axis=-1, keepdims=True)).astype(BF16) for s in scores]
    summed = [
        dot(e, jnp.concatenate([values[p], ones], axis=1)) for e, p in zip(exponent, pieces)
    ]
    attended = jnp.concatenate(
        [(s[:, :width] * (1.0 / s[:, width:])).astype(BF16) for s in summed], axis=0
    )
    residual = flat + dot(attended, out)
    again = rms(residual, gain).astype(BF16)
    hidden = gelu(dot(again, up)).astype(BF16)
    return (residual + dot(hidden, down)).astype(BF16)


def main_kernel(
    state_hbm, visc_hbm, lift_hbm, bias_hbm, gains_hbm, query_hbm, key_hbm, value_hbm, out_hbm,
    up_hbm, down_hbm, head_hbm,
    s3, eddy,
    s0, s1, s2, visc, nu_f, nu_b, nu_sum, xs, xr, ys, yr, zs, zr, pool, filt, recv, hid, cbuf,
    ebuf, lift_w, bias_w, gains_w, query_w, key_w, value_w, out_w, up_w, down_w, head_w,
    load_sem, weight_sem, face_send, face_recv, a_send, a_recv, b_send, b_recv, edge_send,
):
    gx, gy, gz = lax.axis_index("gx"), lax.axis_index("gy"), lax.axis_index("gz")
    plane = gx * 2 + gy
    others = peers(gx, gy)
    loads = []
    for x in (0, 3, 1, 2):
        for n, (src, dst) in enumerate(((state_hbm, s0), (visc_hbm, visc))):
            loads.append(pltpu.make_async_copy(src.at[:, x], dst.at[x], load_sem.at[n, x]))
            loads[-1].start()

    barrier = pltpu.get_barrier_semaphore()
    z_next, z_last = lax.rem(gz + 1, 4), lax.rem(gz + 3, 4)
    for tx, ty in others:
        pl.semaphore_signal(barrier, inc=1, device_id={"gx": tx, "gy": ty}, device_id_type=MESH)
    for target in (z_next, z_last):
        pl.semaphore_signal(barrier, inc=1, device_id={"gz": target}, device_id_type=MESH)
    pl.semaphore_signal(
        barrier, inc=1, device_id={"gx": 0, "gy": 0, "gz": z_next}, device_id_type=MESH
    )
    pl.semaphore_signal(
        barrier, inc=1, device_id={"gx": 31, "gy": 1, "gz": z_last}, device_id_type=MESH
    )
    for copy in loads[:4]:
        copy.wait()

    lanes32 = iota((32, 128), 1)

    def stage_x(e, source):
        xs[e, 0] = source[0].astype(BF16)
        xs[e, 1] = source[3].astype(BF16)

    def stage_yz(e, source):
        packed = jnp.zeros((32, 128), F32)
        for x in range(4):
            for f in range(4):
                j = x * 4 + f
                ys[e, 0, j : j + 1, :] = source[x, f, 0:1, :]
                ys[e, 1, j : j + 1, :] = source[x, f, 31:32, :]
                block = source[x, f]
                packed = jnp.where(lanes32 == j, block[:, 0:1], packed)
                packed = jnp.where(lanes32 == 16 + j, block[:, 127:128], packed)
        zs[e] = packed

    x_next, x_last = lax.rem(gx + 1, 32), lax.rem(gx + 31, 32)

    def face_copies(e):
        pairs = (
            (xs.at[e, 1], xr.at[e, 0], {"gx": x_next}),
            (xs.at[e, 0], xr.at[e, 1], {"gx": x_last}),
            (zs.at[e], zr.at[e, 0], {"gz": z_next}),
            (zs.at[e], zr.at[e, 1], {"gz": z_last}),
            (ys.at[e], yr.at[e], {"gy": 1 - gy}),
        )
        return [
            pltpu.make_async_remote_copy(
                src_ref=src, dst_ref=dst, send_sem=face_send.at[e, n], recv_sem=face_recv.at[e, n],
                device_id=device, device_id_type=MESH,
            )
            for n, (src, dst, device) in enumerate(pairs)
        ]

    copies = [face_copies(e) for e in range(4)]

    def start_x(e):
        copies[e][0].start()
        copies[e][1].start()

    def start_yz(e):
        for copy in copies[e][2:]:
            copy.start()

    def wait_x(e):
        copies[e][0].wait_recv()
        copies[e][1].wait_recv()

    def wait_yz(e):
        for copy in copies[e][2:]:
            copy.wait_recv()

    stage_x(1, visc)
    stage_x(0, s0)
    extra = jnp.where(plane == 0, 64, 0) + jnp.where(plane == 63, 64, 0)
    pl.semaphore_wait(barrier, 65 + extra)
    for e, source in ((1, visc), (0, s0)):
        start_x(e)
    for copy in loads[4:]:
        copy.wait()
    for e, source in ((1, visc), (0, s0)):
        stage_yz(e, source)
        start_yz(e)
    weight_pairs = (
        (lift_hbm, lift_w), (bias_hbm, bias_w), (gains_hbm, gains_w), (query_hbm, query_w),
        (key_hbm, key_w), (value_hbm, value_w), (out_hbm, out_w), (up_hbm, up_w),
        (down_hbm, down_w), (head_hbm, head_w),
    )
    weight_loads = []
    for n, (src, dst) in enumerate(weight_pairs):
        weight_loads.append(pltpu.make_async_copy(src, dst, weight_sem.at[n]))
        weight_loads[-1].start()


    rows = iota((128, 128), 0)
    lanes = iota((128, 128), 1)
    row32 = lax.rem(rows, 32)

    def neighbours(e, source, x):
        middle = source[x].reshape(128, 128)
        if x == 0:
            x_b = xr[e, 0].astype(F32).reshape(128, 128)
        else:
            x_b = source[x - 1].reshape(128, 128)
        if x == 3:
            x_f = xr[e, 1].astype(F32).reshape(128, 128)
        else:
            x_f = source[x + 1].reshape(128, 128)

        def spread(side):
            return jnp.concatenate(
                [
                    jnp.broadcast_to(yr[e, side, x * 4 + f : x * 4 + f + 1, :], (32, 128))
                    for f in range(4)
                ],
                axis=0,
            )

        y_b = jnp.where(row32 == 0, spread(1), pltpu.roll(middle, 1, 0))
        y_f = jnp.where(row32 == 31, spread(0), pltpu.roll(middle, 127, 0))

        def column(side, first):
            return jnp.concatenate(
                [
                    jnp.broadcast_to(
                        zr[e, side, :, first + x * 4 + f : first + x * 4 + f + 1], (32, 128)
                    )
                    for f in range(4)
                ],
                axis=0,
            )

        z_b = jnp.where(lanes == 0, column(0, 16), pltpu.roll(middle, 1, 1))
        z_f = jnp.where(lanes == 127, column(1, 0), pltpu.roll(middle, 127, 1))
        return middle, ((x_b, x_f), (y_b, y_f), (z_b, z_f))

    def advance(e, source, combine, planes):
        for x in planes:
            middle, pairs = neighbours(e, source, x)
            total = -middle * nu_sum[x]
            for d, (before, after) in enumerate(pairs):
                half = (0.5 * TIME_STEP) * source[x, d]
                half = jnp.concatenate([half] * 4, axis=0)
                total += after * (nu_f[d, x] - half) + before * (nu_b[d, x] + half)
            combine(x, middle + total)

    def mean_viscosity(planes):
        for x in planes:
            middle, pairs = neighbours(1, visc, x)
            total = jnp.zeros((128, 128), F32)
            for d, (before, after) in enumerate(pairs):
                forward = (0.5 * TIME_STEP) * (middle + after)
                backward = (0.5 * TIME_STEP) * (middle + before)
                nu_f[d, x] = forward
                nu_b[d, x] = backward
                total += forward + backward
            nu_sum[x] = total

    def first(x, value):
        s1[x] = value.reshape(4, 32, 128)

    def second(x, value):
        s2[x] = (0.75 * s0[x].reshape(128, 128) + 0.25 * value).reshape(4, 32, 128)

    def third(x, value):
        s3[:, x] = (s0[x].reshape(128, 128) / 3.0 + (2.0 / 3.0) * value).reshape(4, 32, 128)

    wait_yz(1)
    mean_viscosity((1, 2))
    wait_yz(0)
    advance(0, s0, first, (1, 2))
    wait_x(1)
    mean_viscosity((0, 3))
    wait_x(0)
    advance(0, s0, first, (0, 3))
    for e, source, target, combine in ((2, s1, s2, second), (3, s2, s3, third)):
        stage_x(e, source)
        start_x(e)
        stage_yz(e, source)
        start_yz(e)
        wait_yz(e)
        advance(e, source, combine, (1, 2))
        wait_x(e)
        advance(e, source, combine, (0, 3))

    pick = jnp.where(iota((64, 128), 1) // 2 == iota((64, 128), 0), 0.125, 0.0)
    for x in range(2):
        one, two = (s3[:, 2 * x + i].reshape(128, 128) for i in range(2))
        pool[x, 0:128] = one + two
        pool[x, 128:256] = one * one + two * two
        paired = pool[x, pl.ds(0, 128, stride=2), :] + pool[x, pl.ds(1, 128, stride=2), :]
        filt[:, x, :] = dot_nt(pick, paired, HIGHEST)

    slot = lax.rem(gx // 4, 4) * 8 + gy * 4 + lax.rem(gx, 4)
    for n, (tx, ty) in enumerate(others):
        far = 1 if n < 32 else 0
        pltpu.make_async_remote_copy(
            src_ref=filt.at[tx * 2 + ty], dst_ref=recv.at[far * 32 + slot], send_sem=a_send,
            recv_sem=a_recv.at[far], device_id={"gx": tx, "gy": ty}, device_id_type=MESH,
        ).start()
    recv[pl.ds(slot, 1)] = filt[pl.ds(plane, 1)]

    for copy in weight_loads:
        copy.wait()
    lift_rows = jnp.concatenate(
        [jnp.broadcast_to(lift_w[c : c + 1, :], (16, 128)) for c in range(8)], axis=0
    )
    head_all = head_w[...].astype(F32)
    head_rows = jnp.concatenate(
        [jnp.broadcast_to(head_all[f : f + 1, :], (32, 128)) for f in range(4)], axis=0
    ).astype(BF16)

    a_near, a_far = (
        pltpu.make_async_remote_copy(
            src_ref=filt.at[pl.ds(0, n)], dst_ref=recv.at[pl.ds(0, n)], send_sem=a_send,
            recv_sem=a_recv.at[far], device_id={"gy": 1 - gy}, device_id_type=MESH,
        )
        for far, n in ((0, 31), (1, 32))
    )

    def block_weights(i):
        return (query_w[i], key_w[i], value_w[i], out_w[i], up_w[i], down_w[i])

    def gain(i):
        return gains_w[i : i + 1, :]

    lift_parts = split(lift_rows, 3)
    lift_pairs = [
        jnp.concatenate([lift_parts[i], lift_parts[j]], axis=0)
        for i, j in ((0, 0), (1, 1), (2, 0))
    ]
    lane16 = lax.rem(iota((64, 256), 1), 16)
    own_y = [jnp.where(lane16 == y, 1.0, 0.0).astype(BF16) for y in range(16)]

    def make_features(far):
        cells = slice(far * 32, far * 32 + 32)
        filtered = jnp.concatenate([recv[cells, 0, :], recv[cells, 1, :]], axis=0)
        one, two, three = split(filtered, 3)
        wide = jnp.concatenate([one, two], axis=1)
        last = jnp.concatenate([one, three], axis=1)
        wide = jnp.concatenate([wide * m for m in own_y], axis=0)
        last = jnp.concatenate([last * m for m in own_y], axis=0)
        lifted = dot(last, lift_pairs[2]) + dot(wide, lift_pairs[1]) + dot(wide, lift_pairs[0])
        features = gelu(rms(lifted + bias_w[...], gain(0))).astype(BF16).astype(F32)
        return features, project(features, gain(1), block_weights(0))

    a_near.wait_recv()
    near = make_features(0)
    a_far.wait_recv()
    far = make_features(1)
    features, projected = (
        jnp.concatenate(
            [part[y * 64 : y * 64 + 64] for y in range(16) for part in halves], axis=0
        )
        for halves in zip(near, far)
    )
    along_x = lax.rem(rows // 4, 2) == lax.rem(lanes // 4, 2)
    result = mixer(features, projected, along_x, gain(2), block_weights(0))
    for y in range(16):
        part = result[y * 128 : y * 128 + 128].astype(F32)
        for c in range(16):
            hid[c, y] = part[c * 8 : c * 8 + 8]

    along_y = lax.rem(rows, 4) == lax.rem(lanes, 4)
    own_lane = lax.rem(lanes, 32) == lax.rem(rows // 4, 2) * 16 + rows // 8
    z_hi = gx // 16

    def finish(chunks):
        lines = jnp.concatenate([hid[c].reshape(128, 128) for c in chunks], axis=0)
        projected = project(lines, gain(3), block_weights(1))
        result = mixer(lines, projected, along_y, gain(4), block_weights(1))
        final = rms(result.astype(F32), gain(5)).astype(BF16)
        spread = dot_nt(final, head_rows)
        for n, c in enumerate(chunks):
            part = jnp.where(own_lane, spread[n * 128 : n * 128 + 128], 0.0).reshape(16, 8, 128)
            part = jnp.sum(part, axis=0)
            logits = part + pltpu.roll(part, 4, 0)
            coefficient = 0.05 + 0.45 * (1.0 / (1.0 + jnp.exp(-logits)))
            half = 1 - z_hi if c >= 8 else z_hi
            for r in range(4):
                x = 2 * (4 * (c % 4) + r) + c // 4 % 2
                cbuf[pl.ds(half * 32 + (1 + x), 1)] = coefficient[r : r + 1, :].reshape(1, 1, 128)

    finish(range(16))
    cbuf[0] = cbuf[64]
    cbuf[65] = cbuf[1]

    def send_edge(slot, target_z, targets):
        for tx, ty in targets:
            pltpu.make_async_remote_copy(
                src_ref=cbuf.at[pl.ds(2 * tx, 4)], dst_ref=ebuf.at[slot], send_sem=edge_send,
                recv_sem=b_recv, device_id={"gx": tx, "gy": ty, "gz": target_z},
                device_id_type=MESH,
            ).start()

    for half in (slice(0, 32), slice(32, 64)):
        for tx, ty in others[half]:
            pltpu.make_async_remote_copy(
                src_ref=cbuf.at[pl.ds(2 * tx, 4)], dst_ref=ebuf.at[plane + 1], send_sem=b_send,
                recv_sem=b_recv, device_id={"gx": tx, "gy": ty}, device_id_type=MESH,
            ).start()

        @pl.when(plane == 63)
        def _(half=half):
            send_edge(0, z_next, (others + [(gx, gy)])[half])

        @pl.when(plane == 0)
        def _(half=half):
            send_edge(65, z_last, (others + [(gx, gy)])[half])

    ebuf[pl.ds(plane + 1, 1)] = cbuf[pl.ds(2 * gx, 4)].reshape(1, 4, 1, 128)
    ebuf[66:80] = jnp.zeros((14, 4, 1, 128), F32)
    b_all = pltpu.make_async_remote_copy(
        src_ref=ebuf.at[pl.ds(0, 63)], dst_ref=ebuf.at[pl.ds(0, 65)], send_sem=b_send,
        recv_sem=b_recv, device_id={"gy": 1 - gy}, device_id_type=MESH,
    )
    row, column = rows, lanes
    fine = lax.rem(column, 32)
    centre = gy * 16 + fine // 2
    other = lax.rem(centre + 31 + 2 * lax.rem(fine, 2), 32)
    same = row // 32 == column // 32
    along_y = jnp.where(same & (lax.rem(row, 32) == centre), 0.75, 0.0) + jnp.where(
        same & (lax.rem(row, 32) == other), 0.25, 0.0
    )
    row, column = iota((80, 128), 0), iota((80, 128), 1)
    centre = 1 + column // 2
    other = centre - 1 + 2 * lax.rem(column, 2)
    along_z = jnp.where(row == centre, 0.75, 0.0) + jnp.where(row == other, 0.25, 0.0)
    along_y = jnp.concatenate([along_y.astype(BF16)] * 2, axis=0)
    along_z = jnp.concatenate([along_z.astype(BF16)] * 2, axis=0)
    b_all.wait_recv()
    cells = [ebuf[:, x, 0, :] for x in range(4)]
    for x in range(4):
        centre, other = (1, 0, 1, 2, 2, 1, 2, 3)[2 * x : 2 * x + 2]
        mixed = 0.75 * cells[centre] + 0.25 * cells[other]
        wide = dot(jnp.concatenate(split(mixed, 2), axis=1), along_y)
        full = lax.dot_general(
            jnp.concatenate(split(wide, 2), axis=0), along_z, (((0,), (0,)), ((), ())),
            preferred_element_type=F32,
        )
        eddy[:, x] = full.reshape(4, 32, 128)
    for e in range(4):
        for copy in copies[e]:
            copy.wait_send()
    a_near.wait_send()
    a_far.wait_send()
    b_all.wait_send()

    @pl.when((plane == 63) | (plane == 0))
    def _():
        pltpu.make_async_remote_copy(
            src_ref=ebuf.at[pl.ds(0, 64)], dst_ref=ebuf.at[pl.ds(0, 64)], send_sem=edge_send,
            recv_sem=b_recv, device_id={"gy": 1 - gy}, device_id_type=MESH,
        ).wait_send()


def store_kernel(first, second, first_out, second_out, sem):
    copies = [
        pltpu.make_async_copy(first, first_out, sem.at[0]),
        pltpu.make_async_copy(second, second_out, sem.at[1]),
    ]
    for copy in copies:
        copy.start()
    for copy in copies:
        copy.wait()


def per_device(state, visc, lift, bias, gains, query, key, value, out, up, down, head):
    hbm = pl.BlockSpec(memory_space=pl.ANY)
    vmem = pltpu.VMEM
    block = (4, 4, 32, 128)
    weights = (lift, bias.reshape(1, 128), gains, query, key, value, out, up, down, head.T)
    results = pl.pallas_call(
        main_kernel,
        out_shape=(vmem(block, F32), vmem(block, F32)),
        in_specs=[hbm] * 12,
        out_specs=(pl.BlockSpec(memory_space=vmem),) * 2,
        scratch_shapes=[vmem(block, F32)] * 4
        + [
            vmem((3, 4, 128, 128), F32),
            vmem((3, 4, 128, 128), F32),
            vmem((4, 128, 128), F32),
            vmem((4, 2, 4, 32, 128), BF16),
            vmem((4, 2, 4, 32, 128), BF16),
            vmem((4, 2, 16, 128), F32),
            vmem((4, 2, 16, 128), F32),
            vmem((4, 32, 128), F32),
            vmem((4, 2, 32, 128), F32),
            vmem((2, 256, 128), F32),
            vmem((64, 2, 128), F32),
            vmem((64, 2, 128), F32),
            vmem((16, 16, 8, 128), F32),
            vmem((66, 1, 128), F32),
            vmem((80, 4, 1, 128), F32),
        ]
        + [vmem(w.shape, w.dtype) for w in weights]
        + [
            DMA((2, 4)),
            DMA((10,)),
            DMA((4, 5)),
            DMA((4, 5)),
            DMA,
            DMA((2,)),
            DMA,
            DMA,
            DMA,
        ],
        compiler_params=pltpu.CompilerParams(
            collective_id=0, has_side_effects=True, vmem_limit_bytes=60 << 20
        ),
        name="flow_and_columns",
    )(state, visc, *weights)
    return pl.pallas_call(
        store_kernel,
        out_shape=(jax.ShapeDtypeStruct(block, F32),) * 2,
        in_specs=[hbm, hbm],
        out_specs=(hbm, hbm),
        scratch_shapes=[DMA((2,))],
        compiler_params=pltpu.CompilerParams(vmem_limit_bytes=1 << 20),
        name="store",
    )(*results)


def solution(mesh):
    cells = P(None, "gx", "gy", "gz")
    return jax.shard_map(
        per_device,
        mesh=mesh,
        in_specs=(cells, cells) + (P(),) * 10,
        out_specs=(cells, cells),
        check_vma=False,
    )
```

```python
import math

import jax
import jax.numpy as jnp
from jax import lax
from jax.experimental import pallas as pl
from jax.experimental.pallas import tpu as pltpu
from jax.sharding import PartitionSpec as P

EPSILON = 1e-06
TIME_STEP = 0.3
MESH = pl.DeviceIdType.MESH
F32 = jnp.float32
BF16 = jnp.bfloat16
DMA = pltpu.SemaphoreType.DMA
HIGHEST = lax.Precision.HIGHEST


def iota(shape, dim):
    return lax.broadcasted_iota(jnp.int32, shape, dim)


def split(values, count):
    parts = []
    for _ in range(count):
        parts.append(values.astype(BF16))
        values = values - parts[-1].astype(F32)
    return parts


def rms(values, gain):
    square = jnp.mean(values * values, axis=-1, keepdims=True)
    return values * lax.rsqrt(square + EPSILON) * gain


def gelu(values):
    inner = math.sqrt(2.0 / math.pi) * (values + 0.044715 * (values * values * values))
    return 0.5 * values * (1.0 + jnp.tanh(inner))


def dot(left, right):
    return jnp.dot(left, right, preferred_element_type=F32)


def dot_nt(left, right, precision=None):
    return lax.dot_general(
        left, right, (((1,), (1,)), ((), ())), precision=precision, preferred_element_type=F32
    )


def peers(gx, gy):
    z, x, y = gx // 16, lax.rem(gx // 4, 4), lax.rem(gx, 4)

    def ring(place):
        return [(lax.rem(place + n, 4), min(n, 4 - n)) for n in (2, 1, 3, 0)]

    found = [
        (dx + dy, tz * 16 + tx * 4 + ty, tc)
        for tx, dx in ring(x)
        for ty, dy in ring(y)
        for tz in (1 - z, z)
        for tc in (1 - gy, gy)
    ]
    return [(place, core) for _, place, core in sorted(found, key=lambda found: -found[0])]


def project(flat, gain, weights):
    query, key, value = weights[:3]
    normed = rms(flat, gain).astype(BF16)
    return dot(normed, jnp.concatenate([query, key, value], axis=1)).astype(BF16)


def mixer(flat, projected, mask, gain, weights):
    width = flat.shape[1]
    pieces = [slice(g * 128, g * 128 + 128) for g in range(flat.shape[0] // 128)]
    out, up, down = weights[3:]
    queries = projected[:, :width]
    keys = projected[:, width : 2 * width]
    values = projected[:, 2 * width :]
    ones = jnp.ones((128, width), BF16)
    scores = [
        jnp.where(mask, dot_nt(queries[p], keys[p]), -1e30) * (width**-0.5) for p in pieces
    ]
    exponent = [jnp.exp(s - jnp.max(s, axis=-1, keepdims=True)).astype(BF16) for s in scores]
    summed = [
        dot(e, jnp.concatenate([values[p], ones], axis=1)) for e, p in zip(exponent, pieces)
    ]
    attended = jnp.concatenate(
        [(s[:, :width] * (1.0 / s[:, width:])).astype(BF16) for s in summed], axis=0
    )
    residual = flat + dot(attended, out)
    again = rms(residual, gain).astype(BF16)
    hidden = gelu(dot(again, up)).astype(BF16)
    return (residual + dot(hidden, down)).astype(BF16)


def main_kernel(
    state_hbm, visc_hbm, lift_hbm, bias_hbm, gains_hbm, query_hbm, key_hbm, value_hbm, out_hbm,
    up_hbm, down_hbm, head_hbm,
    s3, eddy,
    s0, s1, s2, visc, nu_f, nu_b, nu_sum, xs, xr, ys, yr, zs, zr, pool, filt, recv, hid, cbuf,
    ebuf, lift_w, bias_w, gains_w, query_w, key_w, value_w, out_w, up_w, down_w, head_w,
    load_sem, weight_sem, face_send, face_recv, a_send, a_recv, b_send, b_recv, edge_send,
):
    gx, gy, gz = lax.axis_index("gx"), lax.axis_index("gy"), lax.axis_index("gz")
    plane = gx * 2 + gy
    others = peers(gx, gy)
    loads = []
    for x in (0, 3, 1, 2):
        for n, (src, dst) in enumerate(((state_hbm, s0), (visc_hbm, visc))):
            loads.append(pltpu.make_async_copy(src.at[:, x], dst.at[x], load_sem.at[n, x]))
            loads[-1].start()

    barrier = pltpu.get_barrier_semaphore()
    z_next, z_last = lax.rem(gz + 1, 4), lax.rem(gz + 3, 4)
    x_next, x_last = lax.rem(gx + 1, 32), lax.rem(gx + 31, 32)
    z_kept = lax.rem(gz + 2, 4)
    greeted = [{"gx": tx, "gy": ty, "gz": z_kept} for tx, ty in others]
    greeted += [{"gx": x_next}, {"gx": x_last}, {"gz": z_next}, {"gz": z_last}, {"gy": 1 - gy}]
    greeted += [{"gx": 31, "gy": 1, "gz": z_next}, {"gx": 0, "gy": 0, "gz": z_last}]
    for device in greeted:
        pl.semaphore_signal(barrier, inc=1, device_id=device, device_id_type=MESH)

    for copy in loads[:4]:
        copy.wait()

    lanes32 = iota((32, 128), 1)

    def stage_x(e, source):
        xs[e, 0] = source[0].astype(BF16)
        xs[e, 1] = source[3].astype(BF16)

    def stage_yz(e, source):
        packed = jnp.zeros((32, 128), F32)
        for x in range(4):
            for f in range(4):
                j = x * 4 + f
                ys[e, 0, j : j + 1, :] = source[x, f, 0:1, :]
                ys[e, 1, j : j + 1, :] = source[x, f, 31:32, :]
                block = source[x, f]
                packed = jnp.where(lanes32 == j, block[:, 0:1], packed)
                packed = jnp.where(lanes32 == 16 + j, block[:, 127:128], packed)
        zs[e] = packed


    def face_copies(e):
        pairs = (
            (xs.at[e, 1], xr.at[e, 0], {"gx": x_next}),
            (xs.at[e, 0], xr.at[e, 1], {"gx": x_last}),
            (zs.at[e], zr.at[e, 0], {"gz": z_next}),
            (zs.at[e], zr.at[e, 1], {"gz": z_last}),
            (ys.at[e], yr.at[e], {"gy": 1 - gy}),
        )
        return [
            pltpu.make_async_remote_copy(
                src_ref=src, dst_ref=dst, send_sem=face_send.at[e, n], recv_sem=face_recv.at[e, n],
                device_id=device, device_id_type=MESH,
            )
            for n, (src, dst, device) in enumerate(pairs)
        ]

    copies = [face_copies(e) for e in range(4)]

    def start_x(e):
        copies[e][0].start()
        copies[e][1].start()

    def start_yz(e):
        for copy in copies[e][2:]:
            copy.start()

    def wait_x(e):
        copies[e][0].wait_recv()
        copies[e][1].wait_recv()

    def wait_yz(e):
        for copy in copies[e][2:]:
            copy.wait_recv()

    stage_x(1, visc)
    stage_x(0, s0)
    extra = jnp.where(plane == 0, 64, 0) + jnp.where(plane == 63, 64, 0)
    pl.semaphore_wait(barrier, 69 + extra)
    for e, source in ((1, visc), (0, s0)):
        start_x(e)
    for copy in loads[4:]:
        copy.wait()
    for e, source in ((1, visc), (0, s0)):
        stage_yz(e, source)
        start_yz(e)
    weight_pairs = (
        (lift_hbm, lift_w), (bias_hbm, bias_w), (gains_hbm, gains_w), (query_hbm, query_w),
        (key_hbm, key_w), (value_hbm, value_w), (out_hbm, out_w), (up_hbm, up_w),
        (down_hbm, down_w), (head_hbm, head_w),
    )
    weight_loads = []
    for n, (src, dst) in enumerate(weight_pairs):
        weight_loads.append(pltpu.make_async_copy(src, dst, weight_sem.at[n]))
        weight_loads[-1].start()


    rows = iota((128, 128), 0)
    lanes = iota((128, 128), 1)
    row32 = lax.rem(rows, 32)

    def neighbours(e, source, x):
        middle = source[x].reshape(128, 128)
        if x == 0:
            x_b = xr[e, 0].astype(F32).reshape(128, 128)
        else:
            x_b = source[x - 1].reshape(128, 128)
        if x == 3:
            x_f = xr[e, 1].astype(F32).reshape(128, 128)
        else:
            x_f = source[x + 1].reshape(128, 128)

        def spread(side):
            return jnp.concatenate(
                [
                    jnp.broadcast_to(yr[e, side, x * 4 + f : x * 4 + f + 1, :], (32, 128))
                    for f in range(4)
                ],
                axis=0,
            )

        y_b = jnp.where(row32 == 0, spread(1), pltpu.roll(middle, 1, 0))
        y_f = jnp.where(row32 == 31, spread(0), pltpu.roll(middle, 127, 0))

        def column(side, first):
            return jnp.concatenate(
                [
                    jnp.broadcast_to(
                        zr[e, side, :, first + x * 4 + f : first + x * 4 + f + 1], (32, 128)
                    )
                    for f in range(4)
                ],
                axis=0,
            )

        z_b = jnp.where(lanes == 0, column(0, 16), pltpu.roll(middle, 1, 1))
        z_f = jnp.where(lanes == 127, column(1, 0), pltpu.roll(middle, 127, 1))
        return middle, ((x_b, x_f), (y_b, y_f), (z_b, z_f))

    def advance(e, source, combine, planes):
        for x in planes:
            middle, pairs = neighbours(e, source, x)
            total = -middle * nu_sum[x]
            for d, (before, after) in enumerate(pairs):
                half = (0.5 * TIME_STEP) * source[x, d]
                half = jnp.concatenate([half] * 4, axis=0)
                total += after * (nu_f[d, x] - half) + before * (nu_b[d, x] + half)
            combine(x, middle + total)

    def mean_viscosity(planes):
        for x in planes:
            middle, pairs = neighbours(1, visc, x)
            total = jnp.zeros((128, 128), F32)
            for d, (before, after) in enumerate(pairs):
                forward = (0.5 * TIME_STEP) * (middle + after)
                backward = (0.5 * TIME_STEP) * (middle + before)
                nu_f[d, x] = forward
                nu_b[d, x] = backward
                total += forward + backward
            nu_sum[x] = total

    def first(x, value):
        s1[x] = value.reshape(4, 32, 128)

    def second(x, value):
        s2[x] = (0.75 * s0[x].reshape(128, 128) + 0.25 * value).reshape(4, 32, 128)

    def third(x, value):
        s3[:, x] = (s0[x].reshape(128, 128) / 3.0 + (2.0 / 3.0) * value).reshape(4, 32, 128)

    wait_yz(1)
    mean_viscosity((1, 2))
    wait_yz(0)
    advance(0, s0, first, (1, 2))
    wait_x(1)
    mean_viscosity((0, 3))
    wait_x(0)
    advance(0, s0, first, (0, 3))
    for e, source, target, combine in ((2, s1, s2, second), (3, s2, s3, third)):
        stage_x(e, source)
        start_x(e)
        stage_yz(e, source)
        start_yz(e)
        wait_yz(e)
        advance(e, source, combine, (1, 2))
        wait_x(e)
        advance(e, source, combine, (0, 3))

    pick = jnp.where(iota((64, 128), 1) // 2 == iota((64, 128), 0), 0.125, 0.0)
    for x in range(2):
        one, two = (s3[:, 2 * x + i].reshape(128, 128) for i in range(2))
        pool[x, 0:128] = one + two
        pool[x, 128:256] = one * one + two * two
        paired = pool[x, pl.ds(0, 128, stride=2), :] + pool[x, pl.ds(1, 128, stride=2), :]
        filt[:, x, :] = dot_nt(pick, paired, HIGHEST)

    chip_x = lax.rem(gx // 4, 4)
    late = 1 - lax.rem((chip_x + 1) // 2, 2)
    slot = late * 32 + (gx // 16 * 2 + chip_x // 2) * 8 + gy * 4 + lax.rem(gx, 4)
    for tx, ty in others:
        pltpu.make_async_remote_copy(
            src_ref=filt.at[tx * 2 + ty], dst_ref=recv.at[slot], send_sem=a_send,
            recv_sem=a_recv.at[late], device_id={"gx": tx, "gy": ty, "gz": z_kept},
            device_id_type=MESH,
        ).start()

    for copy in weight_loads:
        copy.wait()
    lift_rows = jnp.concatenate(
        [jnp.broadcast_to(lift_w[c : c + 1, :], (16, 128)) for c in range(8)], axis=0
    )
    head_all = head_w[...].astype(F32)
    head_rows = jnp.concatenate(
        [jnp.broadcast_to(head_all[f : f + 1, :], (32, 128)) for f in range(4)], axis=0
    ).astype(BF16)

    a_early, a_late = (
        pltpu.make_async_remote_copy(
            src_ref=filt.at[pl.ds(0, 32)], dst_ref=recv.at[pl.ds(0, 32)], send_sem=a_send,
            recv_sem=a_recv.at[half], device_id={"gy": 1 - gy}, device_id_type=MESH,
        )
        for half in range(2)
    )

    def block_weights(i):
        return (query_w[i], key_w[i], value_w[i], out_w[i], up_w[i], down_w[i])

    def gain(i):
        return gains_w[i : i + 1, :]

    lift_parts = split(lift_rows, 3)
    lift_pairs = [
        jnp.concatenate([lift_parts[i], lift_parts[j]], axis=0)
        for i, j in ((0, 0), (1, 1), (2, 0))
    ]
    lane16 = lax.rem(iota((64, 256), 1), 16)
    own_y = [jnp.where(lane16 == y, 1.0, 0.0).astype(BF16) for y in range(16)]

    def make_features(half):
        cells = slice(half * 32, half * 32 + 32)
        filtered = jnp.concatenate([recv[cells, 0, :], recv[cells, 1, :]], axis=0)
        one, two, three = split(filtered, 3)
        wide = jnp.concatenate([one, two], axis=1)
        last = jnp.concatenate([one, three], axis=1)
        wide = jnp.concatenate([wide * m for m in own_y], axis=0)
        last = jnp.concatenate([last * m for m in own_y], axis=0)
        lifted = dot(last, lift_pairs[2]) + dot(wide, lift_pairs[1]) + dot(wide, lift_pairs[0])
        features = gelu(rms(lifted + bias_w[...], gain(0))).astype(BF16).astype(F32)
        return features, project(features, gain(1), block_weights(0))

    a_early.wait_recv()
    early = make_features(0)
    a_late.wait_recv()
    late = make_features(1)
    features, projected = (
        jnp.concatenate(
            [part[y * 64 : y * 64 + 64] for y in range(16) for part in halves], axis=0
        )
        for halves in zip(early, late)
    )
    along_x = lax.rem(rows // 4, 2) == lax.rem(lanes // 4, 2)
    result = mixer(features, projected, along_x, gain(2), block_weights(0))
    for y in range(16):
        part = result[y * 128 : y * 128 + 128].astype(F32)
        for c in range(16):
            hid[c, y] = part[c * 8 : c * 8 + 8]

    along_y = lax.rem(rows, 4) == lax.rem(lanes, 4)
    own_lane = lax.rem(lanes, 32) == lax.rem(rows // 4, 2) * 16 + rows // 8

    def finish(chunks):
        lines = jnp.concatenate([hid[c].reshape(128, 128) for c in chunks], axis=0)
        projected = project(lines, gain(3), block_weights(1))
        result = mixer(lines, projected, along_y, gain(4), block_weights(1))
        final = rms(result.astype(F32), gain(5)).astype(BF16)
        spread = dot_nt(final, head_rows)
        for n, c in enumerate(chunks):
            part = jnp.where(own_lane, spread[n * 128 : n * 128 + 128], 0.0).reshape(16, 8, 128)
            part = jnp.sum(part, axis=0)
            logits = part + pltpu.roll(part, 4, 0)
            coefficient = 0.05 + 0.45 * (1.0 / (1.0 + jnp.exp(-logits)))
            chip = c % 4 // 2 * 4 + (3 * (c % 2) if c >= 8 else 1 + c % 2)
            for r in range(4):
                cbuf[1 + 2 * (4 * chip + r) + c // 4 % 2] = coefficient[r : r + 1, :]

    finish(range(16))
    cbuf[0] = cbuf[64]
    cbuf[65] = cbuf[1]

    def send_edge(slot, target_z, targets):
        for tx, ty in targets:
            pltpu.make_async_remote_copy(
                src_ref=cbuf.at[pl.ds(2 * tx, 4)], dst_ref=ebuf.at[slot], send_sem=edge_send,
                recv_sem=b_recv, device_id={"gx": tx, "gy": ty, "gz": target_z},
                device_id_type=MESH,
            ).start()

    @pl.when(plane == 63)
    def _():
        send_edge(0, z_last, others[:32])

    @pl.when(plane == 0)
    def _():
        send_edge(65, z_next, others[:32])

    for tx, ty in others:
        pltpu.make_async_remote_copy(
            src_ref=cbuf.at[pl.ds(2 * tx, 4)], dst_ref=ebuf.at[plane + 1], send_sem=b_send,
            recv_sem=b_recv, device_id={"gx": tx, "gy": ty, "gz": z_kept}, device_id_type=MESH,
        ).start()

    @pl.when(plane == 63)
    def _():
        send_edge(0, z_last, others[32:])

    @pl.when(plane == 0)
    def _():
        send_edge(65, z_next, others[32:])

    ebuf[66:80] = jnp.zeros((14, 4, 1, 128), F32)
    b_all = pltpu.make_async_remote_copy(
        src_ref=ebuf.at[pl.ds(0, 64)], dst_ref=ebuf.at[pl.ds(0, 66)], send_sem=b_send,
        recv_sem=b_recv, device_id={"gy": 1 - gy}, device_id_type=MESH,
    )
    row, column = rows, lanes
    fine = lax.rem(column, 32)
    centre = gy * 16 + fine // 2
    other = lax.rem(centre + 31 + 2 * lax.rem(fine, 2), 32)
    same = row // 32 == column // 32
    along_y = jnp.where(same & (lax.rem(row, 32) == centre), 0.75, 0.0) + jnp.where(
        same & (lax.rem(row, 32) == other), 0.25, 0.0
    )
    row, column = iota((80, 128), 0), iota((80, 128), 1)
    centre = 1 + column // 2
    other = centre - 1 + 2 * lax.rem(column, 2)
    along_z = jnp.where(row == centre, 0.75, 0.0) + jnp.where(row == other, 0.25, 0.0)
    along_y = jnp.concatenate([along_y.astype(BF16)] * 2, axis=0)
    along_z = jnp.concatenate([along_z.astype(BF16)] * 2, axis=0)
    b_all.wait_recv()
    cells = [ebuf[:, x, 0, :] for x in range(4)]
    for x in range(4):
        centre, other = (1, 0, 1, 2, 2, 1, 2, 3)[2 * x : 2 * x + 2]
        mixed = 0.75 * cells[centre] + 0.25 * cells[other]
        wide = dot(jnp.concatenate(split(mixed, 2), axis=1), along_y)
        full = lax.dot_general(
            jnp.concatenate(split(wide, 2), axis=0), along_z, (((0,), (0,)), ((), ())),
            preferred_element_type=F32,
        )
        eddy[:, x] = full.reshape(4, 32, 128)
    for e in range(4):
        for copy in copies[e]:
            copy.wait_send()
    a_early.wait_send()
    a_late.wait_send()
    b_all.wait_send()

    @pl.when((plane == 63) | (plane == 0))
    def _():
        pltpu.make_async_remote_copy(
            src_ref=ebuf.at[pl.ds(0, 64)], dst_ref=ebuf.at[pl.ds(0, 64)], send_sem=edge_send,
            recv_sem=b_recv, device_id={"gy": 1 - gy}, device_id_type=MESH,
        ).wait_send()


def store_kernel(first, second, first_out, second_out, sem):
    copies = [
        pltpu.make_async_copy(first, first_out, sem.at[0]),
        pltpu.make_async_copy(second, second_out, sem.at[1]),
    ]
    for copy in copies:
        copy.start()
    for copy in copies:
        copy.wait()


def per_device(state, visc, lift, bias, gains, query, key, value, out, up, down, head):
    hbm = pl.BlockSpec(memory_space=pl.ANY)
    vmem = pltpu.VMEM
    block = (4, 4, 32, 128)
    weights = (lift, bias.reshape(1, 128), gains, query, key, value, out, up, down, head.T)
    results = pl.pallas_call(
        main_kernel,
        out_shape=(vmem(block, F32), vmem(block, F32)),
        in_specs=[hbm] * 12,
        out_specs=(pl.BlockSpec(memory_space=vmem),) * 2,
        scratch_shapes=[vmem(block, F32)] * 4
        + [
            vmem((3, 4, 128, 128), F32),
            vmem((3, 4, 128, 128), F32),
            vmem((4, 128, 128), F32),
            vmem((4, 2, 4, 32, 128), BF16),
            vmem((4, 2, 4, 32, 128), BF16),
            vmem((4, 2, 16, 128), F32),
            vmem((4, 2, 16, 128), F32),
            vmem((4, 32, 128), F32),
            vmem((4, 2, 32, 128), F32),
            vmem((2, 256, 128), F32),
            vmem((64, 2, 128), F32),
            vmem((64, 2, 128), F32),
            vmem((16, 16, 8, 128), F32),
            vmem((66, 1, 128), F32),
            vmem((80, 4, 1, 128), F32),
        ]
        + [vmem(w.shape, w.dtype) for w in weights]
        + [
            DMA((2, 4)),
            DMA((10,)),
            DMA((4, 5)),
            DMA((4, 5)),
            DMA,
            DMA((2,)),
            DMA,
            DMA,
            DMA,
        ],
        compiler_params=pltpu.CompilerParams(
            collective_id=0, has_side_effects=True, vmem_limit_bytes=60 << 20
        ),
        name="flow_and_columns",
    )(state, visc, *weights)
    return pl.pallas_call(
        store_kernel,
        out_shape=(jax.ShapeDtypeStruct(block, F32),) * 2,
        in_specs=[hbm, hbm],
        out_specs=(hbm, hbm),
        scratch_shapes=[DMA((2,))],
        compiler_params=pltpu.CompilerParams(vmem_limit_bytes=1 << 20),
        name="store",
    )(*results)


def solution(mesh):
    cells = P(None, "gx", "gy", "gz")
    return jax.shard_map(
        per_device,
        mesh=mesh,
        in_specs=(cells, cells) + (P(),) * 10,
        out_specs=(cells, cells),
        check_vma=False,
    )
```

```python
import math

import jax
import jax.numpy as jnp
from jax import lax
from jax.experimental import pallas as pl
from jax.experimental.pallas import tpu as pltpu
from jax.sharding import PartitionSpec as P

EPSILON = 1e-06
TIME_STEP = 0.3
MESH = pl.DeviceIdType.MESH
F32 = jnp.float32
BF16 = jnp.bfloat16
DMA = pltpu.SemaphoreType.DMA


def iota(shape, dim):
    return lax.broadcasted_iota(jnp.int32, shape, dim)


def split(values, count):
    parts = []
    for _ in range(count):
        parts.append(values.astype(BF16))
        values = values - parts[-1].astype(F32)
    return parts


def rms(values, gain):
    square = jnp.mean(values * values, axis=-1, keepdims=True)
    return values * lax.rsqrt(square + EPSILON) * gain


def gelu(values):
    inner = math.sqrt(2.0 / math.pi) * (values + 0.044715 * (values * values * values))
    return 0.5 * values * (1.0 + jnp.tanh(inner))


def dot(left, right):
    return jnp.dot(left, right, preferred_element_type=F32)


def dot_nt(left, right):
    return lax.dot_general(
        left, right, (((1,), (1,)), ((), ())), preferred_element_type=F32
    )


def peers(gx, gy):
    z, x, y = gx // 16, lax.rem(gx // 4, 4), lax.rem(gx, 4)

    def ring(place):
        return [(lax.rem(place + n, 4), min(n, 4 - n)) for n in (2, 1, 3, 0)]

    found = [
        (dx + dy, tz * 16 + tx * 4 + ty, tc)
        for tx, dx in ring(x)
        for ty, dy in ring(y)
        for tz in (1 - z, z)
        for tc in (1 - gy, gy)
    ]
    return [(place, core) for _, place, core in sorted(found, key=lambda found: -found[0])]


def project(flat, gain, weights):
    query, key, value = weights[:3]
    normed = rms(flat, gain).astype(BF16)
    return dot(normed, jnp.concatenate([query, key, value], axis=1)).astype(BF16)


def mixer(flat, projected, mask, gain, weights):
    width = flat.shape[1]
    pieces = [slice(g * 128, g * 128 + 128) for g in range(flat.shape[0] // 128)]
    out, up, down = weights[3:]
    queries = projected[:, :width]
    keys = projected[:, width : 2 * width]
    values = projected[:, 2 * width :]
    ones = jnp.ones((128, width), BF16)
    scores = [
        jnp.where(mask, dot_nt(queries[p], keys[p]), -1e30) * (width**-0.5) for p in pieces
    ]
    exponent = [jnp.exp(s - jnp.max(s, axis=-1, keepdims=True)).astype(BF16) for s in scores]
    summed = [
        dot(e, jnp.concatenate([values[p], ones], axis=1)) for e, p in zip(exponent, pieces)
    ]
    attended = jnp.concatenate(
        [(s[:, :width] * (1.0 / s[:, width:])).astype(BF16) for s in summed], axis=0
    )
    residual = flat + dot(attended, out)
    again = rms(residual, gain).astype(BF16)
    hidden = gelu(dot(again, up)).astype(BF16)
    return (residual + dot(hidden, down)).astype(BF16)


def main_kernel(
    state_hbm, visc_hbm, lift_hbm, bias_hbm, gains_hbm, query_hbm, key_hbm, value_hbm, out_hbm,
    up_hbm, down_hbm, head_hbm,
    s3, eddy,
    s0, s1, s2, visc, nu_f, nu_b, nu_sum, xs, xr, ys, yr, zs, zr, pool, filt, recv, hid, cbuf,
    ebuf, lift_w, bias_w, gains_w, query_w, key_w, value_w, out_w, up_w, down_w, head_w,
    load_sem, weight_sem, face_send, face_recv, a_send, a_recv, b_send, b_recv, edge_send,
):
    gx, gy, gz = lax.axis_index("gx"), lax.axis_index("gy"), lax.axis_index("gz")
    plane = gx * 2 + gy
    others = peers(gx, gy)
    loads = []
    for x in (0, 3, 1, 2):
        for n, (src, dst) in enumerate(((state_hbm, s0), (visc_hbm, visc))):
            loads.append(pltpu.make_async_copy(src.at[:, x], dst.at[x], load_sem.at[n, x]))
            loads[-1].start()

    barrier = pltpu.get_barrier_semaphore()
    z_next, z_last = lax.rem(gz + 1, 4), lax.rem(gz + 3, 4)
    x_next, x_last = lax.rem(gx + 1, 32), lax.rem(gx + 31, 32)
    z_kept = lax.rem(gz + 2, 4)
    greeted = [{"gx": tx, "gy": ty, "gz": z_kept} for tx, ty in others]
    greeted += [{"gx": x_next}, {"gx": x_last}, {"gz": z_next}, {"gz": z_last}, {"gy": 1 - gy}]
    greeted += [{"gx": 31, "gy": 1, "gz": z_next}, {"gx": 0, "gy": 0, "gz": z_last}]
    for device in greeted:
        pl.semaphore_signal(barrier, inc=1, device_id=device, device_id_type=MESH)

    for copy in loads[:4]:
        copy.wait()

    lanes32 = iota((32, 128), 1)

    def stage_x(e, source):
        xs[e, 0] = source[0].astype(BF16)
        xs[e, 1] = source[3].astype(BF16)

    def stage_yz(e, source):
        packed = jnp.zeros((32, 128), F32)
        for x in range(4):
            for f in range(4):
                j = x * 4 + f
                ys[e, 0, j : j + 1, :] = source[x, f, 0:1, :]
                ys[e, 1, j : j + 1, :] = source[x, f, 31:32, :]
                block = source[x, f]
                packed = jnp.where(lanes32 == j, block[:, 0:1], packed)
                packed = jnp.where(lanes32 == 16 + j, block[:, 127:128], packed)
        zs[e] = sum(pltpu.roll(packed[8 * g : 8 * g + 8], 32 * g, 1) for g in range(1, 4)) + packed[:8]


    def face_copies(e):
        pairs = (
            (xs.at[e, 1], xr.at[e, 0], {"gx": x_next}),
            (xs.at[e, 0], xr.at[e, 1], {"gx": x_last}),
            (zs.at[e], zr.at[e, 0], {"gz": z_next}),
            (zs.at[e], zr.at[e, 1], {"gz": z_last}),
            (ys.at[e], yr.at[e], {"gy": 1 - gy}),
        )
        return [
            pltpu.make_async_remote_copy(
                src_ref=src, dst_ref=dst, send_sem=face_send.at[e, n], recv_sem=face_recv.at[e, n],
                device_id=device, device_id_type=MESH,
            )
            for n, (src, dst, device) in enumerate(pairs)
        ]

    copies = [face_copies(e) for e in range(4)]

    def start_x(e):
        copies[e][0].start()
        copies[e][1].start()

    def start_yz(e):
        for copy in copies[e][2:]:
            copy.start()

    def wait_x(e):
        copies[e][0].wait_recv()
        copies[e][1].wait_recv()

    def wait_yz(e):
        for copy in copies[e][2:]:
            copy.wait_recv()

    stage_x(1, visc)
    stage_x(0, s0)
    extra = jnp.where(plane == 0, 64, 0) + jnp.where(plane == 63, 64, 0)
    pl.semaphore_wait(barrier, 69 + extra)
    for e, source in ((1, visc), (0, s0)):
        start_x(e)
    for copy in loads[4:]:
        copy.wait()
    for e, source in ((1, visc), (0, s0)):
        stage_yz(e, source)
        start_yz(e)
    weight_pairs = (
        (lift_hbm, lift_w), (bias_hbm, bias_w), (gains_hbm, gains_w), (query_hbm, query_w),
        (key_hbm, key_w), (value_hbm, value_w), (out_hbm, out_w), (up_hbm, up_w),
        (down_hbm, down_w), (head_hbm, head_w),
    )
    weight_loads = []
    for n, (src, dst) in enumerate(weight_pairs):
        weight_loads.append(pltpu.make_async_copy(src, dst, weight_sem.at[n]))
        weight_loads[-1].start()


    rows = iota((128, 128), 0)
    lanes = iota((128, 128), 1)
    row32 = lax.rem(rows, 32)

    def neighbours(e, source, x):
        middle = source[x].reshape(128, 128)
        if x == 0:
            x_b = xr[e, 0].astype(F32).reshape(128, 128)
        else:
            x_b = source[x - 1].reshape(128, 128)
        if x == 3:
            x_f = xr[e, 1].astype(F32).reshape(128, 128)
        else:
            x_f = source[x + 1].reshape(128, 128)

        def spread(side):
            return jnp.concatenate(
                [
                    jnp.broadcast_to(yr[e, side, x * 4 + f : x * 4 + f + 1, :], (32, 128))
                    for f in range(4)
                ],
                axis=0,
            )

        y_b = jnp.where(row32 == 0, spread(1), pltpu.roll(middle, 1, 0))
        y_f = jnp.where(row32 == 31, spread(0), pltpu.roll(middle, 127, 0))

        def column(side, first):
            return jnp.concatenate(
                [
                    jnp.broadcast_to(zr[e, side, :, place : place + 1], (8, 128))
                    for f in range(4)
                    for place in range(first + x * 4 + f, 128, 32)
                ],
                axis=0,
            )

        z_b = jnp.where(lanes == 0, column(0, 16), pltpu.roll(middle, 1, 1))
        z_f = jnp.where(lanes == 127, column(1, 0), pltpu.roll(middle, 127, 1))
        return middle, ((x_b, x_f), (y_b, y_f), (z_b, z_f))

    def advance(e, source, combine, planes):
        for x in planes:
            middle, pairs = neighbours(e, source, x)
            total = -middle * nu_sum[x]
            for d, (before, after) in enumerate(pairs):
                half = (0.5 * TIME_STEP) * source[x, d]
                half = jnp.concatenate([half] * 4, axis=0)
                total += after * (nu_f[d, x] - half) + before * (nu_b[d, x] + half)
            combine(x, middle + total)

    def mean_viscosity(planes):
        for x in planes:
            middle, pairs = neighbours(1, visc, x)
            total = jnp.zeros((128, 128), F32)
            for d, (before, after) in enumerate(pairs):
                forward = (0.5 * TIME_STEP) * (middle + after)
                backward = (0.5 * TIME_STEP) * (middle + before)
                nu_f[d, x] = forward
                nu_b[d, x] = backward
                total += forward + backward
            nu_sum[x] = total

    def first(x, value):
        s1[x] = value.reshape(4, 32, 128)

    def second(x, value):
        s2[x] = (0.75 * s0[x].reshape(128, 128) + 0.25 * value).reshape(4, 32, 128)

    def third(x, value):
        s3[:, x] = (s0[x].reshape(128, 128) / 3.0 + (2.0 / 3.0) * value).reshape(4, 32, 128)

    wait_yz(1)
    mean_viscosity((1, 2))
    wait_yz(0)
    advance(0, s0, first, (1, 2))
    wait_x(1)
    mean_viscosity((0, 3))
    wait_x(0)
    advance(0, s0, first, (0, 3))
    for e, source, target, combine in ((2, s1, s2, second), (3, s2, s3, third)):
        stage_x(e, source)
        start_x(e)
        stage_yz(e, source)
        start_yz(e)
        wait_yz(e)
        advance(e, source, combine, (1, 2))
        wait_x(e)
        advance(e, source, combine, (0, 3))

    pick = jnp.where(iota((64, 128), 1) // 2 == iota((64, 128), 0), 0.125, 0.0)
    pick = jnp.concatenate([pick.astype(BF16)] * 3, axis=1)
    for x in range(2):
        one, two = (s3[:, 2 * x + i].reshape(128, 128) for i in range(2))
        pool[x, 0:128] = one + two
        pool[x, 128:256] = one * one + two * two
        paired = pool[x, pl.ds(0, 128, stride=2), :] + pool[x, pl.ds(1, 128, stride=2), :]
        filt[:, x, :] = dot_nt(pick, jnp.concatenate(split(paired, 3), axis=1))

    z_hi, chip_x, chip_y = gx // 16, lax.rem(gx // 4, 4), lax.rem(gx, 4)
    outer = 1 - lax.rem((chip_x + 1) // 2, 2)
    late = outer * (1 - lax.rem(chip_x // 2 + chip_y // 2, 2))
    group = (1 - late) * (z_hi * 3 + (1 - outer) * (chip_x - 1) + outer * 2) + late * (6 + z_hi)
    slot = group * 8 + gy * 4 + lax.rem(chip_y + 2 * outer * (1 - late), 4)
    for tx, ty in others:
        pltpu.make_async_remote_copy(
            src_ref=filt.at[tx * 2 + ty], dst_ref=recv.at[slot], send_sem=a_send,
            recv_sem=a_recv.at[late], device_id={"gx": tx, "gy": ty, "gz": z_kept},
            device_id_type=MESH,
        ).start()

    for copy in weight_loads:
        copy.wait()
    lift_rows = jnp.concatenate(
        [jnp.broadcast_to(lift_w[c : c + 1, :], (16, 128)) for c in range(8)], axis=0
    )
    head_all = head_w[...].astype(F32)
    head_rows = jnp.concatenate(
        [jnp.broadcast_to(head_all[f : f + 1, :], (32, 128)) for f in range(4)], axis=0
    ).astype(BF16)

    a_early, a_late = (
        pltpu.make_async_remote_copy(
            src_ref=filt.at[pl.ds(0, n)], dst_ref=recv.at[pl.ds(0, n)], send_sem=a_send,
            recv_sem=a_recv.at[part], device_id={"gy": 1 - gy}, device_id_type=MESH,
        )
        for part, n in ((0, 48), (1, 16))
    )

    def block_weights(i):
        return (query_w[i], key_w[i], value_w[i], out_w[i], up_w[i], down_w[i])

    def gain(i):
        return gains_w[i : i + 1, :]

    lift_parts = split(lift_rows, 3)
    lift_pairs = [
        jnp.concatenate([lift_parts[i], lift_parts[j]], axis=0)
        for i, j in ((0, 0), (1, 1), (2, 0))
    ]
    lane16 = lax.rem(iota((32, 256), 1), 16)
    own_y = [jnp.where(lane16 == y, 1.0, 0.0).astype(BF16) for y in range(16)]

    def make_features(cells):
        filtered = jnp.concatenate([recv[cells, 0, :], recv[cells, 1, :]], axis=0)
        repeat = filtered.shape[0] // 32
        one, two, three = split(filtered, 3)
        wide = jnp.concatenate([one, two], axis=1)
        last = jnp.concatenate([one, three], axis=1)
        wide = jnp.concatenate([wide * jnp.concatenate([m] * repeat, axis=0) for m in own_y], axis=0)
        last = jnp.concatenate([last * jnp.concatenate([m] * repeat, axis=0) for m in own_y], axis=0)
        lifted = dot(last, lift_pairs[2]) + dot(wide, lift_pairs[1]) + dot(wide, lift_pairs[0])
        features = gelu(rms(lifted + bias_w[...], gain(0))).astype(BF16).astype(F32)
        return features, project(features, gain(1), block_weights(0))

    a_early.wait_recv()
    early = make_features(slice(0, 48))
    a_late.wait_recv()
    last = make_features(slice(48, 64))
    features, projected = (
        jnp.concatenate(
            [
                part[y * n : y * n + n]
                for y in range(16)
                for part, n in zip(parts, (96, 32))
            ],
            axis=0,
        )
        for parts in zip(early, last)
    )
    along_x = lax.rem(rows // 4, 2) == lax.rem(lanes // 4, 2)
    result = mixer(features, projected, along_x, gain(2), block_weights(0))
    for y in range(16):
        part = result[y * 128 : y * 128 + 128].astype(F32)
        for c in range(16):
            hid[c, y] = part[c * 8 : c * 8 + 8]

    along_y = lax.rem(rows, 4) == lax.rem(lanes, 4)
    own_lane = lax.rem(lanes, 32) == lax.rem(rows // 4, 2) * 16 + rows // 8

    def finish(chunks):
        lines = jnp.concatenate([hid[c].reshape(128, 128) for c in chunks], axis=0)
        projected = project(lines, gain(3), block_weights(1))
        result = mixer(lines, projected, along_y, gain(4), block_weights(1))
        final = rms(result.astype(F32), gain(5)).astype(BF16)
        spread = dot_nt(final, head_rows)
        for n, c in enumerate(chunks):
            part = jnp.where(own_lane, spread[n * 128 : n * 128 + 128], 0.0).reshape(16, 8, 128)
            part = jnp.sum(part, axis=0)
            logits = part + pltpu.roll(part, 4, 0)
            coefficient = 0.05 + 0.45 * (1.0 / (1.0 + jnp.exp(-logits)))
            parity, group = (c // 6, c % 6) if c < 12 else (c % 4 // 2, 6 + c % 2)
            for r in range(4):
                if group >= 6:
                    place = (group - 6) * 16 + (0, 1, 14, 15)[r]
                else:
                    place = group // 3 * 16 + ((4, 5, 6, 7), (8, 9, 10, 11), (2, 3, 12, 13))[
                        group % 3
                    ][r]
                cbuf[1 + 2 * place + parity] = coefficient[r : r + 1, :]

    finish(range(16))
    cbuf[0] = cbuf[64]
    cbuf[65] = cbuf[1]

    def send_edge(slot, target_z, targets):
        for tx, ty in targets:
            pltpu.make_async_remote_copy(
                src_ref=cbuf.at[pl.ds(2 * tx, 4)], dst_ref=ebuf.at[slot], send_sem=edge_send,
                recv_sem=b_recv, device_id={"gx": tx, "gy": ty, "gz": target_z},
                device_id_type=MESH,
            ).start()

    @pl.when(plane == 63)
    def _():
        send_edge(0, z_last, others[:32])

    @pl.when(plane == 0)
    def _():
        send_edge(65, z_next, others[:32])

    for tx, ty in others:
        pltpu.make_async_remote_copy(
            src_ref=cbuf.at[pl.ds(2 * tx, 4)], dst_ref=ebuf.at[plane + 1], send_sem=b_send,
            recv_sem=b_recv, device_id={"gx": tx, "gy": ty, "gz": z_kept}, device_id_type=MESH,
        ).start()

    @pl.when(plane == 63)
    def _():
        send_edge(0, z_last, others[32:])

    @pl.when(plane == 0)
    def _():
        send_edge(65, z_next, others[32:])

    ebuf[66:80] = jnp.zeros((14, 4, 1, 128), F32)
    b_all = pltpu.make_async_remote_copy(
        src_ref=ebuf.at[pl.ds(0, 64)], dst_ref=ebuf.at[pl.ds(0, 66)], send_sem=b_send,
        recv_sem=b_recv, device_id={"gy": 1 - gy}, device_id_type=MESH,
    )
    row, column = rows, lanes
    fine = lax.rem(column, 32)
    centre = gy * 16 + fine // 2
    other = lax.rem(centre + 31 + 2 * lax.rem(fine, 2), 32)
    same = row // 32 == column // 32
    along_y = jnp.where(same & (lax.rem(row, 32) == centre), 0.75, 0.0) + jnp.where(
        same & (lax.rem(row, 32) == other), 0.25, 0.0
    )
    row, column = iota((80, 128), 0), iota((80, 128), 1)
    centre = 1 + column // 2
    other = centre - 1 + 2 * lax.rem(column, 2)
    along_z = jnp.where(row == centre, 0.75, 0.0) + jnp.where(row == other, 0.25, 0.0)
    along_y = jnp.concatenate([along_y.astype(BF16)] * 2, axis=0)
    along_z = jnp.concatenate([along_z.astype(BF16)] * 2, axis=0)
    b_all.wait_recv()
    cells = [ebuf[:, x, 0, :] for x in range(4)]
    for x in range(4):
        centre, other = (1, 0, 1, 2, 2, 1, 2, 3)[2 * x : 2 * x + 2]
        mixed = 0.75 * cells[centre] + 0.25 * cells[other]
        wide = dot(jnp.concatenate(split(mixed, 2), axis=1), along_y)
        full = lax.dot_general(
            jnp.concatenate(split(wide, 2), axis=0), along_z, (((0,), (0,)), ((), ())),
            preferred_element_type=F32,
        )
        eddy[:, x] = full.reshape(4, 32, 128)
    for e in range(4):
        for copy in copies[e]:
            copy.wait_send()
    a_early.wait_send()
    a_late.wait_send()
    b_all.wait_send()

    @pl.when((plane == 63) | (plane == 0))
    def _():
        pltpu.make_async_remote_copy(
            src_ref=ebuf.at[pl.ds(0, 64)], dst_ref=ebuf.at[pl.ds(0, 64)], send_sem=edge_send,
            recv_sem=b_recv, device_id={"gy": 1 - gy}, device_id_type=MESH,
        ).wait_send()


def store_kernel(first, second, first_out, second_out, sem):
    copies = [
        pltpu.make_async_copy(first, first_out, sem.at[0]),
        pltpu.make_async_copy(second, second_out, sem.at[1]),
    ]
    for copy in copies:
        copy.start()
    for copy in copies:
        copy.wait()


def per_device(state, visc, lift, bias, gains, query, key, value, out, up, down, head):
    hbm = pl.BlockSpec(memory_space=pl.ANY)
    vmem = pltpu.VMEM
    block = (4, 4, 32, 128)
    weights = (lift, bias.reshape(1, 128), gains, query, key, value, out, up, down, head.T)
    results = pl.pallas_call(
        main_kernel,
        out_shape=(vmem(block, F32), vmem(block, F32)),
        in_specs=[hbm] * 12,
        out_specs=(pl.BlockSpec(memory_space=vmem),) * 2,
        scratch_shapes=[vmem(block, F32)] * 4
        + [
            vmem((3, 4, 128, 128), F32),
            vmem((3, 4, 128, 128), F32),
            vmem((4, 128, 128), F32),
            vmem((4, 2, 4, 32, 128), BF16),
            vmem((4, 2, 4, 32, 128), BF16),
            vmem((4, 2, 16, 128), F32),
            vmem((4, 2, 16, 128), F32),
            vmem((4, 8, 128), F32),
            vmem((4, 2, 8, 128), F32),
            vmem((2, 256, 128), F32),
            vmem((64, 2, 128), F32),
            vmem((64, 2, 128), F32),
            vmem((16, 16, 8, 128), F32),
            vmem((66, 1, 128), F32),
            vmem((80, 4, 1, 128), F32),
        ]
        + [vmem(w.shape, w.dtype) for w in weights]
        + [
            DMA((2, 4)),
            DMA((10,)),
            DMA((4, 5)),
            DMA((4, 5)),
            DMA,
            DMA((2,)),
            DMA,
            DMA,
            DMA,
        ],
        compiler_params=pltpu.CompilerParams(
            collective_id=0, has_side_effects=True, vmem_limit_bytes=60 << 20
        ),
        name="flow_and_columns",
    )(state, visc, *weights)
    return pl.pallas_call(
        store_kernel,
        out_shape=(jax.ShapeDtypeStruct(block, F32),) * 2,
        in_specs=[hbm, hbm],
        out_specs=(hbm, hbm),
        scratch_shapes=[DMA((2,))],
        compiler_params=pltpu.CompilerParams(vmem_limit_bytes=1 << 20),
        name="store",
    )(*results)


def solution(mesh):
    cells = P(None, "gx", "gy", "gz")
    return jax.shard_map(
        per_device,
        mesh=mesh,
        in_specs=(cells, cells) + (P(),) * 10,
        out_specs=(cells, cells),
        check_vma=False,
    )
```
